128 devices in a mesh: lev: 8 (over x, core), gy: 16 (over z, y).
Axes of the slice: x: 4, y: 4, z: 4, core: 2. Of those that a mesh axis runs over, the one named last changes fastest.
Arguments:
- forcing: bfloat16 [8, 32, 1536, 1024], P('lev', None, 'gy'), may hold values from -6 to 6
- spectral_weight: bfloat16 [2, 128, 32, 32, 128], P(None, 'gy'), may hold values from -4.1875 to 4.1875
- point_weight: bfloat16 [32, 32], replicated, may hold values from -1 to 1
- point_bias: float32 [32], replicated, may hold values from -3 to 3
- decoder: bfloat16 [4, 32], replicated, may hold values from -1 to 1
- coriolis: float32 [1536], P('gy'), may hold values from -1.5 to 1.5
- layer_depth: float32 [8], replicated, may hold values from 0.5 to 2
Outputs:
- equilibrium: float32 [8, 32, 1536, 1024], P('lev', None, 'gy')
- residual: float32 [3, 8, 1536, 1024], P(None, 'lev', 'gy')
The draws below stay inside these ranges and needn't reach their ends.
All inputs are finite; a program needn't handle non-finite values.
Results may differ from the reference program's by a relative error of at most 0.015.
Values may be sent and summed in bfloat16 or wider, within the bound.
A program may use at most 128 MiB of HBM per device.

```python
import math
import jax
import jax.numpy as jnp
from jax import lax

C = 32
NX = 1024
MX = 128
MY = 128
ITERS = 3
LEV = 8
NY = 1536


def levels(key, extent, split, least, top_value):
    def one(axis_at, parts):
        draws = jax.random.uniform(jax.random.fold_in(jax.random.fold_in(key, 6), axis_at), (parts,), jnp.float32, least / len(split), top_value / len(split))
        return jnp.repeat(jnp.exp(draws), extent[axis_at] // parts).reshape((-1,) + (1,) * (len(extent) - axis_at - 1))

    level = one(*split[0])
    for cut in split[1:]:
        level = level * one(*cut)
    return level


def normal_values(rng, extent, deviation, most, cuts=(), kind=jnp.bfloat16):
    entries = jax.random.normal(rng, extent, jnp.float32) * deviation
    if len(cuts) > 0:
        entries = levels(rng, extent, cuts, -0.22, 0.18) * entries
    return jnp.clip(entries, min=-most, max=most).astype(kind)


def setup_inputs(seed: int = 0) -> dict:
    key_list = jax.random.split(jax.random.key(seed), 8)
    forcing = normal_values(key_list[0], (LEV, C, NY, NX), 1.0, 6.0, ((0, 8), (2, 16)))
    spectral_weight = normal_values(key_list[1], (2, MX, C, C, MY), 0.7, 4.1875, ((1, 16),))
    point_weight = normal_values(key_list[2], (C, C), C ** -0.5, 1.0)
    point_bias = normal_values(key_list[3], (C,), 0.5, 3.0, (), jnp.float32)
    decoder = normal_values(key_list[4], (4, C), C ** -0.5, 1.0)
    coriolis = jnp.clip(jax.random.uniform(key_list[5], (NY,), jnp.float32, -1.5, 1.5) * levels(key_list[5], (NY,), ((0, 16),), -0.4, 0.0), -1.5, 1.5)
    layer_depth = jnp.clip(jnp.exp(jax.random.uniform(key_list[6], (LEV,), jnp.float32, math.log(0.5), math.log(2.0))), 0.5, 2.0)
    return {"forcing": forcing, "spectral_weight": spectral_weight, "point_weight": point_weight, "point_bias": point_bias, "decoder": decoder, "coriolis": coriolis, "layer_depth": layer_depth}


def angles(row_index, col_index, length):
    phase = (row_index[:, None] * col_index[None, :]) % length
    return phase.astype(jnp.float32) * (2.0 * math.pi / length)


def signed_modes(length, count):
    index = jnp.arange(count, dtype=jnp.int32)
    return jnp.where(index < count // 2, index, index + (length - count)).astype(jnp.int32)


def forward_x(length, count):
    turned = angles(jnp.arange(length, dtype=jnp.int32), jnp.arange(count, dtype=jnp.int32), length)
    return jnp.stack([jnp.cos(turned), -jnp.sin(turned)], 0).astype(jnp.bfloat16)


def forward_y(row_index, length, count):
    turned = angles(row_index, signed_modes(length, count), length)
    cosine = jnp.cos(turned)
    sine = jnp.sin(turned)
    return jnp.stack([jnp.stack([cosine, -sine], 1), jnp.stack([sine, cosine], 1)], 0).astype(jnp.bfloat16)


def inverse_y(row_index, length, count):
    turned = angles(signed_modes(length, count), row_index, length)
    cosine = jnp.cos(turned)
    sine = jnp.sin(turned)
    return jnp.stack([jnp.stack([cosine, sine], 1), jnp.stack([-sine, cosine], 1)], 0).astype(jnp.bfloat16)


def inverse_x(length, count, total):
    index = jnp.arange(count, dtype=jnp.int32)
    turned = angles(index, jnp.arange(length, dtype=jnp.int32), length)
    factor = jnp.where(index == 0, 1.0, 2.0).astype(jnp.float32)[:, None] / total
    return jnp.stack([factor * jnp.cos(turned), -factor * jnp.sin(turned)], 0).astype(jnp.bfloat16)


def mix_modes(spectrum, weights):
    real_part = spectrum[:, :, 0]
    imag_part = spectrum[:, :, 1]
    weight_real = weights[0].astype(jnp.float32)
    weight_imag = weights[1].astype(jnp.float32)
    highest = lax.Precision.HIGHEST
    out_real = jnp.einsum('klim,kiom->klom', real_part, weight_real, precision=highest) - jnp.einsum('klim,kiom->klom', imag_part, weight_imag, precision=highest)
    out_imag = jnp.einsum('klim,kiom->klom', real_part, weight_imag, precision=highest) + jnp.einsum('klim,kiom->klom', imag_part, weight_real, precision=highest)
    return jnp.stack([out_real, out_imag], 2).astype(jnp.bfloat16)


def product(form, left, right):
    return jnp.einsum(form, left.astype(jnp.float32), right.astype(jnp.float32), precision=lax.Precision.HIGHEST)


def shift_diff(field, axis):
    return (jnp.roll(field, -1, axis) - jnp.roll(field, 1, axis)) * 0.5


def reference(forcing, spectral_weight, point_weight, point_bias, decoder, coriolis, layer_depth):
    row_index = jnp.arange(NY, dtype=jnp.int32)
    table_fx = forward_x(NX, MX)
    table_fy = forward_y(row_index, NY, MY)
    table_iy = inverse_y(row_index, NY, MY)
    table_ix = inverse_x(NX, MX, NX * NY)
    offset = point_bias.astype(jnp.float32)[None, :, None, None]

    def level_step(pair):
        current, source = pair
        current = current[None]
        source = source[None]
        near_modes = product('lcyx,rxk->lrcky', current, table_fx).astype(jnp.bfloat16)
        spectrum = product('lrcky,ryqm->klqcm', near_modes, table_fy)
        mixed = mix_modes(spectrum, spectral_weight)
        back_rows = product('klqcm,qmry->lrcky', mixed, table_iy).astype(jnp.bfloat16)
        spread = product('lrcky,rkx->lcyx', back_rows, table_ix)
        pointwise = product('lcyx,co->loyx', current, point_weight)
        updated = jax.nn.gelu(spread + pointwise + offset + source.astype(jnp.float32), approximate=True)
        return updated[0]

    current = forcing
    for iteration in range(ITERS - 1):
        current = lax.map(level_step, (current, forcing)).astype(jnp.bfloat16)
    final_state = lax.map(level_step, (current, forcing))

    def decode_level(level_state):
        return product('cyx,fc->fyx', level_state, decoder)

    fields = lax.map(decode_level, final_state)
    east_wind = fields[:, 0]
    north_wind = fields[:, 1]
    upward = fields[:, 2]
    heat = fields[:, 3]
    geopotential = jnp.cumsum(layer_depth[:, None, None] * heat, axis=0)
    below_level = jnp.concatenate([jnp.zeros_like(upward[:1]), upward[:-1]], 0)
    turning = coriolis[:, None]
    continuity = shift_diff(east_wind, 2) + shift_diff(north_wind, 1) + upward - below_level
    balance_x = turning * north_wind - shift_diff(geopotential, 2)
    balance_y = turning * east_wind + shift_diff(geopotential, 1)
    return final_state, jnp.stack([continuity, balance_x, balance_y], 0)
```

```python
import functools
import math

import jax
import jax.numpy as jnp
import numpy as np
from jax import lax
from jax.experimental import pallas as pl
from jax.experimental.pallas import tpu as pltpu
from jax.sharding import PartitionSpec as P

C = 32
NX = 1024
NY = 1536
M = 128
ROWS = 96
ITERS = 3
MESH = pl.DeviceIdType.MESH
BF = jnp.bfloat16
F32 = jnp.float32
YC = 32
TILE = 256


def turns(a, b, length):
    phase = (a[:, None] * b[None, :]) % length
    return phase.astype(np.float32) * np.float32(2.0 * math.pi / length)


def lane_modes(half, order):
    p, r, s, j = np.meshgrid(np.array(order), np.arange(2), np.arange(4), np.arange(8), indexing="ij")
    k = 32 * s + 8 * p + j if half == 0 else 32 * p + 8 * s + j
    return k.reshape(-1), r.reshape(-1)


@functools.lru_cache(None)
def x_tables():
    forward, inverse = [], []
    for half in range(2):
        for order in ((0, 1, 2, 3), (1, 0, 3, 2)):
            k, r = lane_modes(half, order)
            turned = turns(np.arange(NX), k, NX)
            wave = np.where(r == 0, np.cos(turned), -np.sin(turned)).astype(np.float32)
            factor = np.where(k == 0, 1.0, 2.0).astype(np.float32) / np.float32(NX * NY)
            forward.append(wave)
            inverse.append((wave * factor[None, :]).T)
    return np.stack(forward).astype(BF), np.stack(inverse).astype(BF)


@functools.lru_cache(None)
def y_tables():
    m = np.arange(M)
    signed = np.where(m < M // 2, m, m + NY - M)
    rows = np.arange(NY)
    turned = turns(rows, signed, NY)
    both = np.concatenate([np.cos(turned), np.sin(turned)], 1).astype(np.float32).astype(BF)
    blocks = both.reshape(4, 4, ROWS, 2 * M)
    first = blocks.reshape(4, 4 * ROWS, 2 * M)
    second = blocks.transpose(1, 0, 2, 3).reshape(4, 4 * ROWS, 2 * M)
    return np.stack([first, second])


def pointwise_matrix(point_weight):
    wt = point_weight.astype(F32).T.reshape(2, 8, 2, C).transpose(0, 2, 1, 3).reshape(C, C)
    full = wt[:, None, :, None] * jnp.eye(16, dtype=F32)[None, :, None, :]
    return full.reshape(C * 16, C * 16).astype(BF)


def decoder_matrix(decoder):
    d = decoder.astype(F32).reshape(4, 2, 8, 2).transpose(0, 1, 3, 2).reshape(4, C)
    full = d[:, None, :, None] * jnp.eye(16, dtype=F32)[None, :, None, :]
    return full.reshape(4 * 16, C * 16).astype(BF)


def gelu(v):
    inner = v * (math.sqrt(2.0 / math.pi) + (math.sqrt(2.0 / math.pi) * 0.044715) * (v * v))
    return (0.5 * v) * (1.0 + jnp.tanh(inner))


def lane_mask(rows):
    return lax.broadcasted_iota(jnp.int32, (rows, 128), 1) < 64


def forward_chunk(load, fwd_ref, near_ref, yc):
    mask = lane_mask(yc)
    for h in range(2):
        outs = []
        for par in range(2):
            lhs = jnp.concatenate([load(16 * h + 2 * pair + par) for pair in range(8)], 0)
            outs.append(jnp.dot(lhs, fwd_ref[2 * h + par], preferred_element_type=F32))
        even, odd = outs
        for pair in range(8):
            rows = slice(pair * yc, (pair + 1) * yc)
            for v in range(2):
                e = even[rows, 128 * v:128 * v + 128]
                o = odd[rows, 128 * v:128 * v + 128]
                near_ref[h, 2 * v, :, 128 * pair:128 * pair + 128] = jnp.where(mask, e, o).astype(BF)
                near_ref[h, 2 * v + 1, :, 128 * pair:128 * pair + 128] = jnp.where(mask, o, e).astype(BF)


def first_body(forcing_ref, fwd_ref, near_ref):
    forward_chunk(lambda c: forcing_ref[c], fwd_ref, near_ref, YC)


def update_chunk(back_ref, state_ref, forcing_ref, kron_ref, bias_ref, inv_ref, sink, yc):
    mask = lane_mask(yc)
    groups = []
    for h in range(2):
        even, odd = [], []
        for pair in range(8):
            b = [back_ref[h, p, :, 128 * pair:128 * pair + 128] for p in range(4)]
            even.append(jnp.concatenate([jnp.where(mask, b[0], b[1]), jnp.where(mask, b[2], b[3])], 1))
            odd.append(jnp.concatenate([jnp.where(mask, b[1], b[0]), jnp.where(mask, b[3], b[2])], 1))
        groups.append(jnp.concatenate(even, 0))
        groups.append(jnp.concatenate(odd, 0))
    for t in range(NX // TILE):
        cols = slice(t * TILE, (t + 1) * TILE)
        mixed = []
        for s in range(yc // 16):
            st = state_ref[:, 16 * s:16 * s + 16, cols].reshape(C * 16, TILE)
            mixed.append(jnp.dot(kron_ref[...], st, preferred_element_type=F32).reshape(4, 8, 16, TILE))
        for g in range(4):
            h, par = g // 2, g % 2
            spread = jnp.dot(groups[g], inv_ref[g, :, cols], preferred_element_type=F32)
            spread = spread.reshape(8, yc, TILE)
            for pair in range(8):
                c = 16 * h + 2 * pair + par
                pw = jnp.concatenate([m[g, pair] for m in mixed], 0)
                v = spread[pair] + pw + (forcing_ref[c, :, cols].astype(F32) + bias_ref[c])
                sink(g, pair, c, cols, gelu(v))


def middle_body(back_ref, state_ref, forcing_ref, kron_ref, bias_ref, fwd_ref, inv_ref, out_ref, near_ref):
    def sink(g, pair, c, cols, value):
        out_ref[c, :, cols] = value.astype(BF)

    update_chunk(back_ref, state_ref, forcing_ref, kron_ref, bias_ref, inv_ref, sink, YC)
    forward_chunk(lambda c: out_ref[c], fwd_ref, near_ref, YC)


def last_body(back_ref, state_ref, forcing_ref, kron_ref, bias_ref, dec_ref, inv_ref, out_ref, fields_ref, hold):
    def sink(g, pair, c, cols, value):
        out_ref[c, :, cols] = value
        hold[8 * g + pair, :, cols] = value.astype(BF)

    update_chunk(back_ref, state_ref, forcing_ref, kron_ref, bias_ref, inv_ref, sink, YC)
    for s in range(YC // 16):
        rows = hold[:, 16 * s:16 * s + 16, :].reshape(C * 16, NX)
        f = jnp.dot(dec_ref[...], rows, preferred_element_type=F32)
        fields_ref[:, 16 * s:16 * s + 16, :] = f.reshape(4, 16, NX)


def rows_spec(lead, yc):
    n = len(lead)
    return pl.BlockSpec((*lead, yc, NX), lambda i: (0,) * n + (i, 0))


def whole_spec(shape):
    return pl.BlockSpec(shape, lambda i: (0,) * len(shape), pipeline_mode=pl.Buffered(1))


SMEM = pl.BlockSpec(memory_space=pltpu.SMEM)
LIMIT = 56 << 20


def first_local(forcing, fwd):
    return pl.pallas_call(
        first_body, name="first_local", grid=(ROWS // YC,),
        in_specs=[rows_spec((C,), YC), whole_spec(fwd.shape)],
        out_specs=rows_spec((2, 4), YC),
        out_shape=jax.ShapeDtypeStruct((2, 4, ROWS, NX), BF),
        compiler_params=pltpu.CompilerParams(vmem_limit_bytes=LIMIT),
    )(forcing, fwd)


def middle_local(back, state, forcing, kron, bias, fwd, inv):
    return pl.pallas_call(
        middle_body, name="middle_local", grid=(ROWS // YC,),
        in_specs=[rows_spec((2, 4), YC), rows_spec((C,), YC), rows_spec((C,), YC), whole_spec(kron.shape), SMEM,
                  whole_spec(fwd.shape), whole_spec(inv.shape)],
        out_specs=[rows_spec((C,), YC), rows_spec((2, 4), YC)],
        out_shape=[jax.ShapeDtypeStruct((C, ROWS, NX), BF), jax.ShapeDtypeStruct((2, 4, ROWS, NX), BF)],
        compiler_params=pltpu.CompilerParams(vmem_limit_bytes=LIMIT),
    )(back, state, forcing, kron, bias, fwd, inv)


def last_local(back, state, forcing, kron, bias, dec, inv):
    return pl.pallas_call(
        last_body, name="last_local", grid=(ROWS // YC,),
        in_specs=[rows_spec((2, 4), YC), rows_spec((C,), YC), rows_spec((C,), YC), whole_spec(kron.shape), SMEM,
                  whole_spec(dec.shape), whole_spec(inv.shape)],
        out_specs=[rows_spec((C,), YC), rows_spec((4,), YC)],
        out_shape=[jax.ShapeDtypeStruct((C, ROWS, NX), F32), jax.ShapeDtypeStruct((4, ROWS, NX), F32)],
        scratch_shapes=[pltpu.VMEM((C, YC, NX), BF)],
        compiler_params=pltpu.CompilerParams(vmem_limit_bytes=LIMIT),
    )(back, state, forcing, kron, bias, dec, inv)


def mode_body(near_ref, weight_ref, ytab_ref, back_ref, wbuf, tabs, r1, part, s2, r2, sp, mx, r3, s4,
              wsem, ss, rs):
    g = lax.axis_index("gy")
    z, y = g // 4, g % 4
    own = ((y, z), (z, y))

    def first_peer(h, a):
        return {"gy": z * 4 + a} if h == 0 else {"gy": a * 4 + y}

    def second_peer(h, b):
        return {"gy": b * 4 + y} if h == 0 else {"gy": z * 4 + b}

    barrier = pltpu.get_barrier_semaphore()
    for h in range(2):
        for d in range(1, 4):
            pl.semaphore_signal(barrier, 1, device_id=first_peer(h, (own[h][0] + d) % 4), device_id_type=MESH)
    weights = pltpu.make_async_copy(weight_ref, wbuf, wsem.at[0])
    weights.start()
    tables = [pltpu.make_async_copy(ytab_ref.at[h, own[h][1]], tabs.at[h], wsem.at[1 + h]) for h in range(2)]
    for t in tables:
        t.start()
    pl.semaphore_wait(barrier, 6)

    def exchange(step, h, peer, src, dst):
        copies = []
        for d in range(1, 4):
            c = pltpu.make_async_remote_copy(
                src_ref=src(d), dst_ref=dst(d), send_sem=ss.at[step, h, d - 1], recv_sem=rs.at[step, h, d - 1],
                device_id=peer(d), device_id_type=MESH)
            c.start()
            copies.append(c)
        return copies

    def wait(copies):
        for c in copies:
            c.wait()

    one = []
    for h in range(2):
        a = own[h][0]
        one.append(exchange(0, h, lambda d: first_peer(h, (a + d) % 4),
                            lambda d: near_ref.at[h, (a + d) % 4], lambda d: r1.at[h, a]))
        r1[h, a] = near_ref[h, a]
    two = []
    for h in range(2):
        a, b = own[h]
        tables[h].wait()
        wait(one[h])

        @pl.loop(0, 4)
        def _(n):
            cols = pl.ds(pl.multiple_of(n * 256, 256), 256)
            x = r1[h, :, :, cols].reshape(4 * ROWS, 256)
            cs = lax.dot_general(tabs[h], x, (((0,), (0,)), ((), ())), preferred_element_type=F32)
            pt = cs.T.reshape(2, 2, 2, 4, 8, 256)
            for pair in range(2):
                for h2 in range(2):
                    q0, q1 = pt[pair, h2, 0], pt[pair, h2, 1]
                    re = q0[..., :M] + q1[..., M:]
                    im = q1[..., :M] - q0[..., M:]
                    both = jnp.concatenate([re, im], 1)
                    c = 2 * (2 * n + pair) + lax.rem(h2 + a, 2)
                    part[h, :, c] = both
                    s2[h, :, c] = both.astype(BF)

        two.append(exchange(1, h, lambda d: second_peer(h, (b + d) % 4),
                            lambda d: s2.at[h, (b + d) % 4], lambda d: r2.at[h, d - 1]))
    for h in range(2):
        b = own[h][1]
        wait(two[h])

        @pl.loop(0, 16)
        def _(c):
            total = part[h, b, c]
            for d in range(3):
                total = total + r2[h, d, c].astype(F32)
            sp[16 * h + c] = total

    weights.wait()
    for j in range(8):
        def add(i, acc):
            ar, ai = acc
            wr = wbuf[0, j, i].astype(F32)
            wi = wbuf[1, j, i].astype(F32)
            sr = jnp.broadcast_to(sp[i, pl.ds(j, 1), :], (C, M))
            si = jnp.broadcast_to(sp[i, pl.ds(8 + j, 1), :], (C, M))
            return ar + (sr * wr - si * wi), ai + (sr * wi + si * wr)

        zero = jnp.zeros((C, M), F32)
        ar, ai = lax.fori_loop(0, C, add, (zero, zero), unroll=4)
        mx[pl.ds(j, C, stride=16), :] = ar
        mx[pl.ds(8 + j, C, stride=16), :] = ai
    three = []
    for h in range(2):
        b = own[h][1]
        r3[h, b] = mx[256 * h:256 * h + 256, :].reshape(16, 16, M).astype(BF)
        three.append(exchange(2, h, lambda d: second_peer(h, (b + d) % 4),
                              lambda d: r3.at[h, b], lambda d: r3.at[h, b]))
    four = []
    for h in range(2):
        a = own[h][0]
        wait(three[h])

        @pl.loop(0, 4)
        def _(n):
            rows = []
            for pair in range(2):
                for h2 in range(2):
                    c = 2 * (2 * n + pair) + lax.rem(h2 + a, 2)
                    block = r3[h, :, c].astype(F32).reshape(4, 2, 8, M)
                    re = block[:, 0].reshape(32, M)
                    im = block[:, 1].reshape(32, M)
                    rows.append(jnp.concatenate([re, -im], 1))
                    rows.append(jnp.concatenate([im, re], 1))
            m2 = jnp.concatenate(rows, 0).astype(BF)
            out = lax.dot_general(tabs[h], m2, (((1,), (1,)), ((), ())), preferred_element_type=F32)
            s4[h, :, :, pl.ds(pl.multiple_of(n * 256, 256), 256)] = out.reshape(4, ROWS, 256).astype(BF)

        four.append(exchange(3, h, lambda d: first_peer(h, (a + d) % 4),
                             lambda d: s4.at[h, (a + d) % 4], lambda d: back_ref.at[h, a]))
        back_ref[h, a] = s4[h, a]
    for h in range(2):
        wait(four[h])


def mode_step(near, weights, ytab):
    shape = (2, 4, ROWS, NX)
    return pl.pallas_call(
        mode_body, name="mode_step",
        in_specs=[pl.BlockSpec(memory_space=pltpu.VMEM), pl.BlockSpec(memory_space=pl.ANY),
                  pl.BlockSpec(memory_space=pl.ANY)],
        out_specs=pl.BlockSpec(memory_space=pltpu.VMEM),
        out_shape=jax.ShapeDtypeStruct(shape, BF),
        scratch_shapes=[
            pltpu.VMEM((2, 8, C, C, M), BF),
            pltpu.VMEM((2, 4 * ROWS, 2 * M), BF),
            pltpu.VMEM(shape, BF),
            pltpu.VMEM((2, 4, 16, 16, M), F32),
            pltpu.VMEM((2, 4, 16, 16, M), BF),
            pltpu.VMEM((2, 3, 16, 16, M), BF),
            pltpu.VMEM((C, 16, M), F32),
            pltpu.VMEM((C * 16, M), F32),
            pltpu.VMEM((2, 4, 16, 16, M), BF),
            pltpu.VMEM(shape, BF),
            pltpu.SemaphoreType.DMA((3,)),
            pltpu.SemaphoreType.DMA((4, 2, 3)),
            pltpu.SemaphoreType.DMA((4, 2, 3)),
        ],
        compiler_params=pltpu.CompilerParams(collective_id=1, has_side_effects=True, vmem_limit_bytes=40 << 20),
    )(near, weights, ytab)


def kron_body(row_ref, wt_ref, col_ref, mask_ref, out_ref):
    left = jnp.dot(row_ref[...], wt_ref[...], preferred_element_type=F32).astype(BF)
    full = jnp.dot(left, col_ref[...], preferred_element_type=F32)
    out_ref[...] = (full * mask_ref[...].astype(F32)).astype(BF)


@functools.lru_cache(None)
def kron_parts():
    order = np.arange(C).reshape(2, 8, 2).transpose(0, 2, 1).reshape(C)
    pick = np.zeros((C, C), np.float32)
    pick[np.arange(C), order] = 1.0
    spread = np.repeat(np.eye(C, dtype=np.float32), 16, 1)
    mask = np.tile(np.eye(16, dtype=np.float32), (C, C))
    four = np.repeat(np.eye(4, dtype=np.float32), 16, 0)
    return [v.astype(BF) for v in (np.repeat(pick, 16, 0), spread, mask, four, pick.T @ spread, mask[:64])]


def kron_matrices(point_weight, decoder):
    rows, cols, mask, dec_rows, dec_cols, dec_mask = [jnp.asarray(v) for v in kron_parts()]

    def call(name, a, w, b, m):
        return pl.pallas_call(kron_body, name=name, out_shape=jax.ShapeDtypeStruct(m.shape, BF))(a, w, b, m)

    return call("pointwise_matrix", rows, point_weight.T, cols, mask), call("decoder_matrix", dec_rows, decoder, dec_cols, dec_mask)


def prefix(value, axis):
    peers, place = lax.axis_size(axis), lax.axis_index(axis)
    everything = lax.all_gather(value, axis)
    kept = jnp.where((jnp.arange(peers) < place)[:, None, None], everything, 0.0)
    return jnp.sum(kept, 0)


def roll_diff(field, axis):
    return (jnp.roll(field, -1, axis) - jnp.roll(field, 1, axis)) * 0.5


def residuals(fields, coriolis, layer_depth):
    turning = coriolis[:, None]
    east_wind, north_wind, upward, heat = fields
    own_depth = lax.dynamic_slice_in_dim(layer_depth, lax.axis_index("lev"), 1, 0)
    inside = own_depth[:, None] * heat
    geopotential = inside + prefix(inside, "lev")
    count = lax.axis_size("lev")
    below = lax.ppermute(upward, "lev", [(i, i + 1) for i in range(count - 1)])
    peers = lax.axis_size("gy")
    up = [(i, (i + 1) % peers) for i in range(peers)]
    down = [(j, i) for i, j in up]
    both = jnp.stack([north_wind, geopotential], 0)
    before = lax.ppermute(both[:, -1:], "gy", up)
    after = lax.ppermute(both[:, :1], "gy", down)
    rimmed = jnp.concatenate([before, both, after], 1)
    along_y = (rimmed[:, 2:] - rimmed[:, :-2]) * 0.5
    continuity = roll_diff(east_wind, 1) + along_y[0] + upward - below
    balance_x = turning * north_wind - roll_diff(geopotential, 1)
    balance_y = turning * east_wind + along_y[1]
    return jnp.stack([continuity, balance_x, balance_y], 0)


def on_device(forcing, spectral_weight, point_weight, point_bias, decoder, coriolis, layer_depth):
    source = forcing[0]
    fwd, inv = (jnp.asarray(v) for v in x_tables())
    ytab = jnp.asarray(y_tables())
    kron, dec = kron_matrices(point_weight, decoder)
    near = first_local(source, fwd)
    state = source
    for iteration in range(ITERS - 1):
        back = mode_step(near, spectral_weight, ytab)
        state, near = middle_local(back, state, source, kron, point_bias, fwd, inv)
    back = mode_step(near, spectral_weight, ytab)
    final, fields = last_local(back, state, source, kron, point_bias, dec, inv)
    residual = residuals(fields, coriolis, layer_depth)
    return final[None], residual[:, None]


def solution(mesh):
    return jax.shard_map(
        on_device,
        mesh=mesh,
        in_specs=(
            P("lev", None, "gy", None),
            P(None, "gy", None, None, None),
            P(),
            P(),
            P(),
            P("gy"),
            P(),
        ),
        out_specs=(P("lev", None, "gy", None), P(None, "lev", "gy", None)),
        check_vma=False,
    )
```

```python
import functools
import math

import jax
import jax.numpy as jnp
import numpy as np
from jax import lax
from jax.experimental import pallas as pl
from jax.experimental.pallas import tpu as pltpu
from jax.sharding import PartitionSpec as P

C = 32
NX = 1024
NY = 1536
M = 128
ROWS = 96
ITERS = 3
MESH = pl.DeviceIdType.MESH
BF = jnp.bfloat16
F32 = jnp.float32
YC = 32
TILE = 256


def turns(a, b, length):
    phase = (a[:, None] * b[None, :]) % length
    return phase.astype(np.float32) * np.float32(2.0 * math.pi / length)


def lane_modes(half, order):
    p, r, s, j = np.meshgrid(np.array(order), np.arange(2), np.arange(4), np.arange(8), indexing="ij")
    k = 32 * s + 8 * p + j if half == 0 else 32 * p + 8 * s + j
    return k.reshape(-1), r.reshape(-1)


@functools.lru_cache(None)
def x_tables():
    forward, inverse = [], []
    for half in range(2):
        for order in ((0, 1, 2, 3), (1, 0, 3, 2)):
            k, r = lane_modes(half, order)
            turned = turns(np.arange(NX), k, NX)
            wave = np.where(r == 0, np.cos(turned), -np.sin(turned)).astype(np.float32)
            factor = np.where(k == 0, 1.0, 2.0).astype(np.float32) / np.float32(NX * NY)
            forward.append(wave)
            inverse.append((wave * factor[None, :]).T)
    return np.stack(forward).astype(BF), np.stack(inverse).astype(BF)


@functools.lru_cache(None)
def y_tables():
    m = np.arange(M)
    signed = np.where(m < M // 2, m, m + NY - M)
    rows = np.arange(NY)
    turned = turns(rows, signed, NY)
    both = np.concatenate([np.cos(turned), np.sin(turned)], 1).astype(np.float32).astype(BF)
    blocks = both.reshape(4, 4, ROWS, 2 * M)
    first = blocks.reshape(4, 4 * ROWS, 2 * M)
    second = blocks.transpose(1, 0, 2, 3).reshape(4, 4 * ROWS, 2 * M)
    return np.stack([first, second])


def pointwise_matrix(point_weight):
    wt = point_weight.astype(F32).T.reshape(2, 8, 2, C).transpose(0, 2, 1, 3).reshape(C, C)
    full = wt[:, None, :, None] * jnp.eye(16, dtype=F32)[None, :, None, :]
    return full.reshape(C * 16, C * 16).astype(BF)


def decoder_matrix(decoder):
    d = decoder.astype(F32).reshape(4, 2, 8, 2).transpose(0, 1, 3, 2).reshape(4, C)
    full = d[:, None, :, None] * jnp.eye(16, dtype=F32)[None, :, None, :]
    return full.reshape(4 * 16, C * 16).astype(BF)


def gelu(v):
    inner = v * (math.sqrt(2.0 / math.pi) + (math.sqrt(2.0 / math.pi) * 0.044715) * (v * v))
    return (0.5 * v) * (1.0 + jnp.tanh(inner))


def lane_mask(rows):
    return lax.broadcasted_iota(jnp.int32, (rows, 128), 1) < 64


def forward_chunk(load, fwd_ref, near_ref, yc):
    mask = lane_mask(yc)
    for h in range(2):
        outs = []
        for par in range(2):
            lhs = jnp.concatenate([load(16 * h + 2 * pair + par) for pair in range(8)], 0)
            outs.append(jnp.dot(lhs, fwd_ref[2 * h + par], preferred_element_type=F32))
        even, odd = outs
        for pair in range(8):
            rows = slice(pair * yc, (pair + 1) * yc)
            for v in range(2):
                e = even[rows, 128 * v:128 * v + 128]
                o = odd[rows, 128 * v:128 * v + 128]
                near_ref[h, 2 * v, :, 128 * pair:128 * pair + 128] = jnp.where(mask, e, o).astype(BF)
                near_ref[h, 2 * v + 1, :, 128 * pair:128 * pair + 128] = jnp.where(mask, o, e).astype(BF)


def first_body(forcing_ref, fwd_ref, near_ref):
    forward_chunk(lambda c: forcing_ref[c], fwd_ref, near_ref, YC)


def update_chunk(back_ref, state_ref, forcing_ref, kron_ref, bias_ref, inv_ref, sink, yc):
    mask = lane_mask(yc)
    groups = []
    for h in range(2):
        even, odd = [], []
        for pair in range(8):
            b = [back_ref[h, p, :, 128 * pair:128 * pair + 128] for p in range(4)]
            even.append(jnp.concatenate([jnp.where(mask, b[0], b[1]), jnp.where(mask, b[2], b[3])], 1))
            odd.append(jnp.concatenate([jnp.where(mask, b[1], b[0]), jnp.where(mask, b[3], b[2])], 1))
        groups.append(jnp.concatenate(even, 0))
        groups.append(jnp.concatenate(odd, 0))
    for t in range(NX // TILE):
        cols = slice(t * TILE, (t + 1) * TILE)
        mixed = []
        for s in range(yc // 16):
            st = state_ref[:, 16 * s:16 * s + 16, cols].reshape(C * 16, TILE)
            mixed.append(jnp.dot(kron_ref[...], st, preferred_element_type=F32).reshape(4, 8, 16, TILE))
        for g in range(4):
            h, par = g // 2, g % 2
            spread = jnp.dot(groups[g], inv_ref[g, :, cols], preferred_element_type=F32)
            spread = spread.reshape(8, yc, TILE)
            for pair in range(8):
                c = 16 * h + 2 * pair + par
                pw = jnp.concatenate([m[g, pair] for m in mixed], 0)
                v = spread[pair] + pw + (forcing_ref[c, :, cols].astype(F32) + bias_ref[c])
                sink(g, pair, c, cols, gelu(v))


def middle_body(back_ref, state_ref, forcing_ref, kron_ref, bias_ref, fwd_ref, inv_ref, out_ref, near_ref):
    def sink(g, pair, c, cols, value):
        out_ref[c, :, cols] = value.astype(BF)

    update_chunk(back_ref, state_ref, forcing_ref, kron_ref, bias_ref, inv_ref, sink, YC)
    forward_chunk(lambda c: out_ref[c], fwd_ref, near_ref, YC)


def last_body(back_ref, state_ref, forcing_ref, kron_ref, bias_ref, dec_ref, inv_ref, out_ref, fields_ref, hold):
    def sink(g, pair, c, cols, value):
        out_ref[c, :, cols] = value
        hold[8 * g + pair, :, cols] = value.astype(BF)

    update_chunk(back_ref, state_ref, forcing_ref, kron_ref, bias_ref, inv_ref, sink, YC)
    for s in range(YC // 16):
        rows = hold[:, 16 * s:16 * s + 16, :].reshape(C * 16, NX)
        f = jnp.dot(dec_ref[...], rows, preferred_element_type=F32)
        fields_ref[:, 16 * s:16 * s + 16, :] = f.reshape(4, 16, NX)


def rows_spec(lead, yc):
    n = len(lead)
    return pl.BlockSpec((*lead, yc, NX), lambda i: (0,) * n + (i, 0))


def whole_spec(shape):
    return pl.BlockSpec(shape, lambda i: (0,) * len(shape), pipeline_mode=pl.Buffered(1))


SMEM = pl.BlockSpec(memory_space=pltpu.SMEM)
LIMIT = 56 << 20


def first_local(forcing, fwd):
    return pl.pallas_call(
        first_body, name="first_local", grid=(ROWS // YC,),
        in_specs=[rows_spec((C,), YC), whole_spec(fwd.shape)],
        out_specs=rows_spec((2, 4), YC),
        out_shape=jax.ShapeDtypeStruct((2, 4, ROWS, NX), BF),
        compiler_params=pltpu.CompilerParams(vmem_limit_bytes=LIMIT),
    )(forcing, fwd)


def middle_local(back, state, forcing, kron, bias, fwd, inv):
    return pl.pallas_call(
        middle_body, name="middle_local", grid=(ROWS // YC,),
        in_specs=[rows_spec((2, 4), YC), rows_spec((C,), YC), rows_spec((C,), YC), whole_spec(kron.shape), SMEM,
                  whole_spec(fwd.shape), whole_spec(inv.shape)],
        out_specs=[rows_spec((C,), YC), rows_spec((2, 4), YC)],
        out_shape=[jax.ShapeDtypeStruct((C, ROWS, NX), BF), jax.ShapeDtypeStruct((2, 4, ROWS, NX), BF)],
        compiler_params=pltpu.CompilerParams(vmem_limit_bytes=LIMIT),
    )(back, state, forcing, kron, bias, fwd, inv)


def last_local(back, state, forcing, kron, bias, dec, inv):
    return pl.pallas_call(
        last_body, name="last_local", grid=(ROWS // YC,),
        in_specs=[rows_spec((2, 4), YC), rows_spec((C,), YC), rows_spec((C,), YC), whole_spec(kron.shape), SMEM,
                  whole_spec(dec.shape), whole_spec(inv.shape)],
        out_specs=[rows_spec((C,), YC), rows_spec((4,), YC)],
        out_shape=[jax.ShapeDtypeStruct((C, ROWS, NX), F32), jax.ShapeDtypeStruct((4, ROWS, NX), F32)],
        scratch_shapes=[pltpu.VMEM((C, YC, NX), BF)],
        compiler_params=pltpu.CompilerParams(vmem_limit_bytes=LIMIT),
    )(back, state, forcing, kron, bias, dec, inv)


def mode_body(near_ref, weight_ref, ytab_ref, back_ref, wbuf, tabs, r1, part, s2, r2, sp, mx, r3, s4,
              wsem, ss, rs):
    g = lax.axis_index("gy")
    z, y = g // 4, g % 4
    own = ((y, z), (z, y))

    def first_peer(h, a):
        return {"gy": z * 4 + a} if h == 0 else {"gy": a * 4 + y}

    def second_peer(h, b):
        return {"gy": b * 4 + y} if h == 0 else {"gy": z * 4 + b}

    barrier = pltpu.get_barrier_semaphore()
    for h in range(2):
        for d in range(1, 4):
            pl.semaphore_signal(barrier, 1, device_id=first_peer(h, (own[h][0] + d) % 4), device_id_type=MESH)
    weights = pltpu.make_async_copy(weight_ref, wbuf, wsem.at[0])
    weights.start()
    tables = [pltpu.make_async_copy(ytab_ref.at[h, own[h][1]], tabs.at[h], wsem.at[1 + h]) for h in range(2)]
    for t in tables:
        t.start()
    pl.semaphore_wait(barrier, 6)

    def exchange(step, h, peer, src, dst):
        copies = []
        for d in range(1, 4):
            c = pltpu.make_async_remote_copy(
                src_ref=src(d), dst_ref=dst(d), send_sem=ss.at[step, h, d - 1], recv_sem=rs.at[step, h, d - 1],
                device_id=peer(d), device_id_type=MESH)
            c.start()
            copies.append(c)
        return copies

    def wait(copies):
        for c in copies:
            c.wait()

    one = []
    for h in range(2):
        a = own[h][0]
        one.append(exchange(0, h, lambda d: first_peer(h, (a + d) % 4),
                            lambda d: near_ref.at[h, (a + d) % 4], lambda d: r1.at[h, a]))
        r1[h, a] = near_ref[h, a]
    two = []
    for h in range(2):
        a, b = own[h]
        tables[h].wait()
        wait(one[h])

        @pl.loop(0, 4)
        def _(n):
            cols = pl.ds(pl.multiple_of(n * 256, 256), 256)
            x = r1[h, :, :, cols].reshape(4 * ROWS, 256)
            cs = lax.dot_general(tabs[h], x, (((0,), (0,)), ((), ())), preferred_element_type=F32)
            pt = cs.T.reshape(2, 2, 2, 4, 8, 256)
            for pair in range(2):
                for h2 in range(2):
                    q0, q1 = pt[pair, h2, 0], pt[pair, h2, 1]
                    re = q0[..., :M] + q1[..., M:]
                    im = q1[..., :M] - q0[..., M:]
                    both = jnp.concatenate([re, im], 1)
                    c = 2 * (2 * n + pair) + lax.rem(h2 + a, 2)
                    part[h, :, c] = both
                    s2[h, :, c] = both.astype(BF)

        two.append(exchange(1, h, lambda d: second_peer(h, (b + d) % 4),
                            lambda d: s2.at[h, (b + d) % 4], lambda d: r2.at[h, d - 1]))
    for h in range(2):
        b = own[h][1]
        wait(two[h])

        @pl.loop(0, 16)
        def _(c):
            total = part[h, b, c]
            for d in range(3):
                total = total + r2[h, d, c].astype(F32)
            sp[16 * h + c] = total

    weights.wait()
    for j in range(8):
        def add(i, acc):
            ar, ai = acc
            wr = wbuf[0, j, i].astype(F32)
            wi = wbuf[1, j, i].astype(F32)
            sr = jnp.broadcast_to(sp[i, pl.ds(j, 1), :], (C, M))
            si = jnp.broadcast_to(sp[i, pl.ds(8 + j, 1), :], (C, M))
            return ar + (sr * wr - si * wi), ai + (sr * wi + si * wr)

        zero = jnp.zeros((C, M), F32)
        ar, ai = lax.fori_loop(0, C, add, (zero, zero), unroll=4)
        mx[pl.ds(j, C, stride=16), :] = ar
        mx[pl.ds(8 + j, C, stride=16), :] = ai
    three = []
    for h in range(2):
        b = own[h][1]
        r3[h, b] = mx[256 * h:256 * h + 256, :].reshape(16, 16, M).astype(BF)
        three.append(exchange(2, h, lambda d: second_peer(h, (b + d) % 4),
                              lambda d: r3.at[h, b], lambda d: r3.at[h, b]))
    four = []
    for h in range(2):
        a = own[h][0]
        wait(three[h])

        @pl.loop(0, 4)
        def _(n):
            rows = []
            for pair in range(2):
                for h2 in range(2):
                    c = 2 * (2 * n + pair) + lax.rem(h2 + a, 2)
                    block = r3[h, :, c].astype(F32).reshape(4, 2, 8, M)
                    re = block[:, 0].reshape(32, M)
                    im = block[:, 1].reshape(32, M)
                    rows.append(jnp.concatenate([re, -im], 1))
                    rows.append(jnp.concatenate([im, re], 1))
            m2 = jnp.concatenate(rows, 0).astype(BF)
            out = lax.dot_general(tabs[h], m2, (((1,), (1,)), ((), ())), preferred_element_type=F32)
            s4[h, :, :, pl.ds(pl.multiple_of(n * 256, 256), 256)] = out.reshape(4, ROWS, 256).astype(BF)

        four.append(exchange(3, h, lambda d: first_peer(h, (a + d) % 4),
                             lambda d: s4.at[h, (a + d) % 4], lambda d: back_ref.at[h, a]))
        back_ref[h, a] = s4[h, a]
    for h in range(2):
        wait(four[h])


def mode_step(near, weights, ytab):
    shape = (2, 4, ROWS, NX)
    return pl.pallas_call(
        mode_body, name="mode_step",
        in_specs=[pl.BlockSpec(memory_space=pltpu.VMEM), pl.BlockSpec(memory_space=pl.ANY),
                  pl.BlockSpec(memory_space=pl.ANY)],
        out_specs=pl.BlockSpec(memory_space=pltpu.VMEM),
        out_shape=jax.ShapeDtypeStruct(shape, BF),
        scratch_shapes=[
            pltpu.VMEM((2, 8, C, C, M), BF),
            pltpu.VMEM((2, 4 * ROWS, 2 * M), BF),
            pltpu.VMEM(shape, BF),
            pltpu.VMEM((2, 4, 16, 16, M), F32),
            pltpu.VMEM((2, 4, 16, 16, M), BF),
            pltpu.VMEM((2, 3, 16, 16, M), BF),
            pltpu.VMEM((C, 16, M), F32),
            pltpu.VMEM((C * 16, M), F32),
            pltpu.VMEM((2, 4, 16, 16, M), BF),
            pltpu.VMEM(shape, BF),
            pltpu.SemaphoreType.DMA((3,)),
            pltpu.SemaphoreType.DMA((4, 2, 3)),
            pltpu.SemaphoreType.DMA((4, 2, 3)),
        ],
        compiler_params=pltpu.CompilerParams(collective_id=1, has_side_effects=True, vmem_limit_bytes=40 << 20),
    )(near, weights, ytab)


def shifted(field, step, axis):
    return pltpu.roll(field, step % field.shape[axis], axis)


def diff_x(field):
    return (shifted(field, -1, 1) - shifted(field, 1, 1)) * 0.5


def diff_y(field, before, after):
    at = lax.broadcasted_iota(jnp.int32, field.shape, 0)
    upper = jnp.where(at == field.shape[0] - 1, after, shifted(field, -1, 0))
    lower = jnp.where(at == 0, before, shifted(field, 1, 0))
    return (upper - lower) * 0.5


def tail_body(fields_ref, turning_ref, depth_ref, out_ref, own, other, chip, lower, total, share, up_out, up_in,
              geo, edge_out, edge_in, ss, rs):
    lev = lax.axis_index("lev")
    g = lax.axis_index("gy")
    x, c = lev // 2, lev % 2
    partner = {"lev": 2 * x + 1 - c}
    next_row, last_row = {"gy": (g + 1) % 16}, {"gy": (g + 15) % 16}
    beside = {"lev": (lev + 1 + 6 * (1 - c)) % 8}
    barrier = pltpu.get_barrier_semaphore()
    for peer in [partner, beside, next_row, last_row] + [{"lev": (lev + 2 * d) % 8} for d in range(1, 4)]:
        pl.semaphore_signal(barrier, 1, device_id=peer, device_id_type=MESH)

    def copy(src, dst, at, peer):
        return pltpu.make_async_remote_copy(src_ref=src, dst_ref=dst, send_sem=ss.at[at], recv_sem=rs.at[at],
                                            device_id=peer, device_id_type=MESH)

    half = pl.ds(pl.multiple_of(48 * c, 48), 48)
    rest = pl.ds(pl.multiple_of(48 * (1 - c), 48), 48)
    weighted = fields_ref[3] * depth_ref[lev]
    own[...] = weighted.astype(BF)
    up_out[...] = fields_ref[2].astype(BF)
    edge_out[0] = fields_ref[1, 88:96]
    edge_out[1] = fields_ref[1, 0:8]
    pl.semaphore_wait(barrier, 7)
    all_rows = copy(own, other, 0, partner)
    some_rows = copy(own.at[0:48], other.at[0:48], 0, partner)

    @pl.when(c == 0)
    def _():
        all_rows.start()

    @pl.when(c == 1)
    def _():
        some_rows.start()

    winds = [copy(edge_out.at[0], edge_in.at[0], 1, next_row), copy(edge_out.at[1], edge_in.at[1], 2, last_row)]
    for w in winds:
        w.start()

    @pl.when(c == 0)
    def _():
        all_rows.wait_send()
        some_rows.wait_recv()

    @pl.when(c == 1)
    def _():
        some_rows.wait_send()
        all_rows.wait_recv()

    chip[...] = (own[half, :].astype(F32) + other[half, :].astype(F32)).astype(BF)
    sums = [copy(chip, lower.at[d - 1], 2 + d, {"lev": (lev + 2 * d) % 8}) for d in range(1, 4)]
    for d in range(1, 4):
        @pl.when(x + d <= 3)
        def _():
            sums[d - 1].start()

    rising = copy(up_out, up_in, 6, {"lev": (lev + 1) % 8})

    @pl.when(lev < 7)
    def _():
        rising.start()

    for w in winds:
        w.wait()
    east, north = fields_ref[0], fields_ref[1]
    out_ref[0] = diff_x(east) + diff_y(north, edge_in[0, 7:8], edge_in[1, 0:1]) + fields_ref[2]
    total[half, :] = jnp.zeros((48, NX), F32)
    for d in range(1, 4):
        @pl.when(x >= d)
        def _():
            sums[d - 1].wait_recv()
            total[half, :] += lower[d - 1].astype(F32)

    share[...] = total[half, :]
    shared = copy(share, total.at[half], 7, partner)
    shared.start()

    @pl.when(lev >= 1)
    def _():
        rising.wait_recv()
        out_ref[0] -= up_in[...].astype(F32)

    shared.wait()
    geo[...] = total[...] + fields_ref[3] * depth_ref[lev]

    @pl.when(c == 1)
    def _():
        geo[...] += other[...].astype(F32)

    edges = [copy(geo.at[88:96], edge_in.at[2], 8, next_row), copy(geo.at[0:8], edge_in.at[3], 9, last_row)]
    for e in edges:
        e.start()
    out_ref[1] = turning_ref[...] * north - diff_x(geo[...])
    for e in edges:
        e.wait()
    out_ref[2] = turning_ref[...] * east + diff_y(geo[...], edge_in[2, 7:8], edge_in[3, 0:1])
    for d in range(1, 4):
        @pl.when(x + d <= 3)
        def _():
            sums[d - 1].wait_send()

    @pl.when(lev < 7)
    def _():
        rising.wait_send()


def tail_step(fields, coriolis, layer_depth):
    vmem = pl.BlockSpec(memory_space=pltpu.VMEM)
    rows = (ROWS, NX)
    return pl.pallas_call(
        tail_body, name="tail_step", in_specs=[vmem, vmem, SMEM], out_specs=vmem,
        out_shape=jax.ShapeDtypeStruct((3, *rows), F32),
        scratch_shapes=[
            pltpu.VMEM(rows, BF), pltpu.VMEM(rows, BF), pltpu.VMEM((48, NX), BF), pltpu.VMEM((3, 48, NX), BF),
            pltpu.VMEM(rows, F32), pltpu.VMEM((48, NX), F32), pltpu.VMEM(rows, BF), pltpu.VMEM(rows, BF),
            pltpu.VMEM(rows, F32), pltpu.VMEM((2, 8, NX), F32), pltpu.VMEM((4, 8, NX), F32),
            pltpu.SemaphoreType.DMA((10,)), pltpu.SemaphoreType.DMA((10,)),
        ],
        compiler_params=pltpu.CompilerParams(collective_id=2, has_side_effects=True, vmem_limit_bytes=24 << 20),
    )(fields, coriolis[:, None], layer_depth)


def kron_body(row_ref, wt_ref, col_ref, mask_ref, out_ref):
    left = jnp.dot(row_ref[...], wt_ref[...], preferred_element_type=F32).astype(BF)
    full = jnp.dot(left, col_ref[...], preferred_element_type=F32)
    out_ref[...] = (full * mask_ref[...].astype(F32)).astype(BF)


@functools.lru_cache(None)
def kron_parts():
    order = np.arange(C).reshape(2, 8, 2).transpose(0, 2, 1).reshape(C)
    pick = np.zeros((C, C), np.float32)
    pick[np.arange(C), order] = 1.0
    spread = np.repeat(np.eye(C, dtype=np.float32), 16, 1)
    mask = np.tile(np.eye(16, dtype=np.float32), (C, C))
    four = np.repeat(np.eye(4, dtype=np.float32), 16, 0)
    return [v.astype(BF) for v in (np.repeat(pick, 16, 0), spread, mask, four, pick.T @ spread, mask[:64])]


def kron_matrices(point_weight, decoder):
    rows, cols, mask, dec_rows, dec_cols, dec_mask = [jnp.asarray(v) for v in kron_parts()]

    def call(name, a, w, b, m):
        return pl.pallas_call(kron_body, name=name, out_shape=jax.ShapeDtypeStruct(m.shape, BF))(a, w, b, m)

    return call("pointwise_matrix", rows, point_weight.T, cols, mask), call("decoder_matrix", dec_rows, decoder, dec_cols, dec_mask)


def on_device(forcing, spectral_weight, point_weight, point_bias, decoder, coriolis, layer_depth):
    source = forcing[0]
    fwd, inv = (jnp.asarray(v) for v in x_tables())
    ytab = jnp.asarray(y_tables())
    kron, dec = kron_matrices(point_weight, decoder)
    near = first_local(source, fwd)
    state = source
    for iteration in range(ITERS - 1):
        back = mode_step(near, spectral_weight, ytab)
        state, near = middle_local(back, state, source, kron, point_bias, fwd, inv)
    back = mode_step(near, spectral_weight, ytab)
    final, fields = last_local(back, state, source, kron, point_bias, dec, inv)
    residual = tail_step(fields, coriolis, layer_depth)
    return final[None], residual[:, None]


def solution(mesh):
    return jax.shard_map(
        on_device,
        mesh=mesh,
        in_specs=(
            P("lev", None, "gy", None),
            P(None, "gy", None, None, None),
            P(),
            P(),
            P(),
            P("gy"),
            P(),
        ),
        out_specs=(P("lev", None, "gy", None), P(None, "lev", "gy", None)),
        check_vma=False,
    )
```

```python
import functools
import math

import jax
import jax.numpy as jnp
import numpy as np
from jax import lax
from jax.experimental import pallas as pl
from jax.experimental.pallas import tpu as pltpu
from jax.sharding import PartitionSpec as P

C = 32
NX = 1024
NY = 1536
M = 128
ROWS = 96
ITERS = 3
MESH = pl.DeviceIdType.MESH
BF = jnp.bfloat16
F32 = jnp.float32
YC = 32
TILE = 256


def turns(a, b, length):
    phase = (a[:, None] * b[None, :]) % length
    return phase.astype(np.float32) * np.float32(2.0 * math.pi / length)


def lane_modes(half, order):
    p, r, s, j = np.meshgrid(np.array(order), np.arange(2), np.arange(4), np.arange(8), indexing="ij")
    k = 32 * s + 8 * p + j if half == 0 else 32 * p + 8 * s + j
    return k.reshape(-1), r.reshape(-1)


@functools.lru_cache(None)
def x_tables():
    forward, inverse = [], []
    for half in range(2):
        for order in ((0, 1, 2, 3), (1, 0, 3, 2)):
            k, r = lane_modes(half, order)
            turned = turns(np.arange(NX), k, NX)
            wave = np.where(r == 0, np.cos(turned), -np.sin(turned)).astype(np.float32)
            factor = np.where(k == 0, 1.0, 2.0).astype(np.float32) / np.float32(NX * NY)
            forward.append(wave)
            inverse.append((wave * factor[None, :]).T)
    return np.stack(forward).astype(BF), np.stack(inverse).astype(BF)


@functools.lru_cache(None)
def y_tables():
    m = np.arange(M)
    signed = np.where(m < M // 2, m, m + NY - M)
    rows = np.arange(NY)
    turned = turns(rows, signed, NY)
    both = np.concatenate([np.cos(turned), np.sin(turned)], 1).astype(np.float32).astype(BF)
    blocks = both.reshape(4, 4, ROWS, 2 * M)
    first = blocks.reshape(4, 4 * ROWS, 2 * M)
    second = blocks.transpose(1, 0, 2, 3).reshape(4, 4 * ROWS, 2 * M)
    return np.stack([first, second])


def gelu(v):
    inner = v * (math.sqrt(2.0 / math.pi) + (math.sqrt(2.0 / math.pi) * 0.044715) * (v * v))
    return (0.5 * v) * (1.0 + jnp.tanh(inner))


def lane_mask(rows):
    return lax.broadcasted_iota(jnp.int32, (rows, 128), 1) < 64


def update_chunk(back_ref, state_ref, forcing_ref, kron_ref, bias_ref, inv_ref, sink, yc):
    mask = lane_mask(yc)
    groups = []
    for h in range(2):
        even, odd = [], []
        for pair in range(8):
            b = [back_ref[h, p, :, 128 * pair:128 * pair + 128] for p in range(4)]
            even.append(jnp.concatenate([jnp.where(mask, b[0], b[1]), jnp.where(mask, b[2], b[3])], 1))
            odd.append(jnp.concatenate([jnp.where(mask, b[1], b[0]), jnp.where(mask, b[3], b[2])], 1))
        groups.append(jnp.concatenate(even, 0))
        groups.append(jnp.concatenate(odd, 0))
    for t in range(NX // TILE):
        cols = slice(t * TILE, (t + 1) * TILE)
        mixed = []
        for s in range(yc // 16):
            st = state_ref[:, 16 * s:16 * s + 16, cols].reshape(C * 16, TILE)
            mixed.append(jnp.dot(kron_ref[...], st, preferred_element_type=F32).reshape(4, 8, 16, TILE))
        for g in range(4):
            h, par = g // 2, g % 2
            spread = jnp.dot(groups[g], inv_ref[g, :, cols], preferred_element_type=F32)
            spread = spread.reshape(8, yc, TILE)
            for pair in range(8):
                c = 16 * h + 2 * pair + par
                pw = jnp.concatenate([m[g, pair] for m in mixed], 0)
                v = spread[pair] + pw + (forcing_ref[c, :, cols].astype(F32) + bias_ref[c])
                sink(g, pair, c, cols, gelu(v))


def last_body(back_ref, state_ref, forcing_ref, pick_ref, wt_ref, cols_ref, bias_ref, four_ref, dec_ref, dcols_ref, inv_ref,
              out_ref, fields_ref, hold, kron_ref, dmat_ref):
    @pl.when(pl.program_id(0) == 0)
    def _():
        kron_ref[...] = kron_values(pick_ref[...], wt_ref[...], cols_ref[...])
        dmat_ref[...] = kron_values(four_ref[...], dec_ref[...], dcols_ref[...])

    def sink(g, pair, c, cols, value):
        out_ref[c, :, cols] = value
        hold[8 * g + pair, :, cols] = value.astype(BF)

    update_chunk(back_ref, state_ref, forcing_ref, kron_ref, bias_ref, inv_ref, sink, YC)
    for s in range(YC // 16):
        rows = hold[:, 16 * s:16 * s + 16, :].reshape(C * 16, NX)
        f = jnp.dot(dmat_ref[...], rows, preferred_element_type=F32)
        fields_ref[:, 16 * s:16 * s + 16, :] = f.reshape(4, 16, NX)


def rows_spec(lead, yc):
    n = len(lead)
    return pl.BlockSpec((*lead, yc, NX), lambda i: (0,) * n + (i, 0))


def whole_spec(shape):
    return pl.BlockSpec(shape, lambda i: (0,) * len(shape), pipeline_mode=pl.Buffered(1))


SMEM = pl.BlockSpec(memory_space=pltpu.SMEM)
LIMIT = 56 << 20


def last_local(back, state, forcing, pick, wt, cols, bias, four, dec, dec_cols, inv):
    return pl.pallas_call(
        last_body, name="last_local", grid=(ROWS // YC,),
        in_specs=[rows_spec((2, 4), YC), rows_spec((C,), YC), rows_spec((C,), YC), whole_spec(pick.shape),
                  whole_spec(wt.shape), whole_spec(cols.shape), SMEM, whole_spec(four.shape), whole_spec(dec.shape),
                  whole_spec(dec_cols.shape), whole_spec(inv.shape)],
        out_specs=[rows_spec((C,), YC), rows_spec((4,), YC)],
        out_shape=[jax.ShapeDtypeStruct((C, ROWS, NX), F32), jax.ShapeDtypeStruct((4, ROWS, NX), F32)],
        scratch_shapes=[pltpu.VMEM((C, YC, NX), BF), pltpu.VMEM((C * 16, C * 16), BF), pltpu.VMEM((64, C * 16), BF)],
        compiler_params=pltpu.CompilerParams(vmem_limit_bytes=LIMIT),
    )(back, state, forcing, pick, wt, cols, bias, four, dec, dec_cols, inv)


def kron_values(rows, weight, cols):
    left = jnp.dot(rows, weight, preferred_element_type=F32).astype(BF)
    full = jnp.dot(left, cols, preferred_element_type=F32)
    i = lax.broadcasted_iota(jnp.int32, full.shape, 0) % 16
    j = lax.broadcasted_iota(jnp.int32, full.shape, 1) % 16
    return jnp.where(i == j, full, 0.0).astype(BF)


def steps_body(forcing_ref, weight_ref, ytab_ref, fwd_hbm, inv_hbm, pick_ref, wt_ref, cols_ref, bias_ref,
               state_out, back_out,
               source, state, fwd, inv, kron, wbuf, tabs, near, r1, part, s2, r2, sp, mx, r3, m2, s4, back,
               lsem, s1s, s1r, s2s, s2r, s3s, s3r, s4s, s4r):
    g = lax.axis_index("gy")
    z, y = g // 4, g % 4
    own = ((y, z), (z, y))

    def first_peer(h, a):
        return {"gy": z * 4 + a} if h == 0 else {"gy": a * 4 + y}

    def second_peer(h, b):
        return {"gy": b * 4 + y} if h == 0 else {"gy": z * 4 + b}

    barrier = pltpu.get_barrier_semaphore()
    for h in range(2):
        for d in range(1, 4):
            pl.semaphore_signal(barrier, 1, device_id=first_peer(h, (own[h][0] + d) % 4), device_id_type=MESH)

    def rows_of(k):
        return pl.ds(pl.multiple_of(k * YC, YC), YC)

    chunks = ROWS // YC

    def local(src, dst, at):
        return pltpu.make_async_copy(src, dst, lsem.at[at])

    load_fwd = local(fwd_hbm, fwd, 0)
    load_source = [local(forcing_ref.at[:, rows_of(k)], source.at[:, rows_of(k)], 1 + k) for k in range(chunks)]
    load_tabs = [local(ytab_ref.at[h, own[h][1]], tabs.at[h], 4 + h) for h in range(2)]
    load_weights = local(weight_ref, wbuf, 6)
    load_inv = local(inv_hbm, inv, 7)
    load_state = local(forcing_ref, state, 8)
    for c in [load_fwd, *load_source, *load_tabs, load_weights, load_inv, load_state]:
        c.start()

    def remote(src, dst, send, recv, peer):
        return pltpu.make_async_remote_copy(src_ref=src, dst_ref=dst, send_sem=send, recv_sem=recv, device_id=peer,
                                            device_id_type=MESH)

    def one(h, d, k):
        a = own[h][0]
        return remote(near.at[h, (a + d) % 4, rows_of(k)], r1.at[h, a, rows_of(k)], s1s.at[h, d - 1, k],
                      s1r.at[h, d - 1, k], first_peer(h, (a + d) % 4))

    def two(h, d):
        b = own[h][1]
        return remote(s2.at[h, (b + d) % 4], r2.at[h, d - 1], s2s.at[h, d - 1], s2r.at[h, d - 1],
                      second_peer(h, (b + d) % 4))

    def three(h, d):
        b = own[h][1]
        return remote(r3.at[h, b], r3.at[h, b], s3s.at[h, d - 1], s3r.at[h, d - 1], second_peer(h, (b + d) % 4))

    def four(h, d, k):
        a = own[h][0]
        return remote(s4.at[h, (a + d) % 4, rows_of(k)], back.at[h, a, rows_of(k)], s4s.at[h, d - 1, k],
                      s4r.at[h, d - 1, k], first_peer(h, (a + d) % 4))

    def forward(k, load):
        rows = rows_of(k)
        mask = lane_mask(YC)
        for h in range(2):
            outs = []
            for par in range(2):
                lhs = jnp.concatenate([load(16 * h + 2 * pair + par, rows) for pair in range(8)], 0)
                outs.append(jnp.dot(lhs, fwd[2 * h + par], preferred_element_type=F32))
            even, odd = outs
            for pair in range(8):
                at = slice(pair * YC, (pair + 1) * YC)
                for v in range(2):
                    e = even[at, 128 * v:128 * v + 128]
                    o = odd[at, 128 * v:128 * v + 128]
                    lanes = slice(128 * pair, 128 * pair + 128)
                    near[h, 2 * v, rows, lanes] = jnp.where(mask, e, o).astype(BF)
                    near[h, 2 * v + 1, rows, lanes] = jnp.where(mask, o, e).astype(BF)
            for d in range(1, 4):
                one(h, d, k).start()
            a = own[h][0]
            r1[h, a, rows] = near[h, a, rows]

    def update(k):
        rows = rows_of(k)
        mask = lane_mask(YC)
        groups = []
        for h in range(2):
            even, odd = [], []
            for pair in range(8):
                b = [back[h, p, rows, 128 * pair:128 * pair + 128] for p in range(4)]
                even.append(jnp.concatenate([jnp.where(mask, b[0], b[1]), jnp.where(mask, b[2], b[3])], 1))
                odd.append(jnp.concatenate([jnp.where(mask, b[1], b[0]), jnp.where(mask, b[3], b[2])], 1))
            groups.append(jnp.concatenate(even, 0))
            groups.append(jnp.concatenate(odd, 0))
        for t in range(NX // TILE):
            cols = slice(t * TILE, (t + 1) * TILE)
            mixed = []
            for s in range(YC // 16):
                at = pl.ds(pl.multiple_of(k * YC + 16 * s, 16), 16)
                st = state[:, at, cols].reshape(C * 16, TILE)
                mixed.append(jnp.dot(kron[...], st, preferred_element_type=F32).reshape(4, 8, 16, TILE))
            for q in range(4):
                h, par = q // 2, q % 2
                spread = jnp.dot(groups[q], inv[q, :, cols], preferred_element_type=F32)
                spread = spread.reshape(8, YC, TILE)
                for pair in range(8):
                    c = 16 * h + 2 * pair + par
                    pw = jnp.concatenate([m[q, pair] for m in mixed], 0)
                    v = spread[pair] + pw + (source[c, rows, cols].astype(F32) + bias_ref[c])
                    state[c, rows, cols] = gelu(v).astype(BF)

    pl.semaphore_wait(barrier, 6)
    load_fwd.wait()
    for k in range(chunks):
        load_source[k].wait()
    pl.loop(0, chunks)(lambda k: forward(k, lambda c, rows: source[c, rows]))
    kron[...] = kron_values(pick_ref[...], wt_ref[...], cols_ref[...])
    for c in [*load_tabs, load_weights, load_inv, load_state]:
        c.wait()

    @pl.loop(0, ITERS)
    def _(it):
        for h in range(2):
            a, b = own[h]
            for k in range(chunks):
                for d in range(1, 4):
                    one(h, d, k).wait()

            @pl.loop(0, 4)
            def _(n):
                cols = pl.ds(pl.multiple_of(n * 256, 256), 256)
                x = r1[h, :, :, cols].reshape(4 * ROWS, 256)
                pt = lax.dot_general(x, tabs[h], (((0,), (0,)), ((), ())), preferred_element_type=F32)
                pt = pt.reshape(2, 2, 2, 4, 8, 256)
                for pair in range(2):
                    for h2 in range(2):
                        q0, q1 = pt[pair, h2, 0], pt[pair, h2, 1]
                        re = q0[..., :M] + q1[..., M:]
                        im = q1[..., :M] - q0[..., M:]
                        both = jnp.concatenate([re, im], 1)
                        c = 2 * (2 * n + pair) + lax.rem(h2 + a, 2)
                        part[h, :, c] = both
                        s2[h, :, c] = both.astype(BF)

            for d in range(1, 4):
                two(h, d).start()
        for h in range(2):
            b = own[h][1]
            for d in range(1, 4):
                two(h, d).wait()

            @pl.loop(0, 16)
            def _(c):
                total = part[h, b, c]
                for d in range(3):
                    total = total + r2[h, d, c].astype(F32)
                sp[16 * h + c] = total

        for oh in range(2):
            b = own[oh][1]
            outs = pl.ds(16 * oh, 16)
            for j in range(8):
                def add(i, acc):
                    ar, ai = acc
                    wr = wbuf[0, j, i, outs].astype(F32)
                    wi = wbuf[1, j, i, outs].astype(F32)
                    sr = jnp.broadcast_to(sp[i, pl.ds(j, 1), :], (16, M))
                    si = jnp.broadcast_to(sp[i, pl.ds(8 + j, 1), :], (16, M))
                    return ar + (sr * wr - si * wi), ai + (sr * wi + si * wr)

                zero = jnp.zeros((16, M), F32)
                ar, ai = lax.fori_loop(0, C, add, (zero, zero), unroll=8)
                mx[pl.ds(j, 16, stride=16), :] = ar
                mx[pl.ds(8 + j, 16, stride=16), :] = ai
            r3[oh, b] = mx[...].reshape(16, 16, M).astype(BF)
            for d in range(1, 4):
                three(oh, d).start()
        for h in range(2):
            a = own[h][0]
            for d in range(1, 4):
                three(h, d).wait()

            @pl.loop(0, 8)
            def _(n):
                rows = []
                for h2 in range(2):
                    c = 2 * n + lax.rem(h2 + a, 2)
                    block = r3[h, :, c].astype(F32).reshape(4, 2, 8, M)
                    re = block[:, 0].reshape(32, M)
                    im = block[:, 1].reshape(32, M)
                    rows.append(jnp.concatenate([re, -im], 1))
                    rows.append(jnp.concatenate([im, re], 1))
                m2[h, pl.ds(pl.multiple_of(n * 128, 128), 128)] = jnp.concatenate(rows, 0).astype(BF)

        @pl.loop(0, chunks)
        def _(k):
            rows = rows_of(k)
            for h in range(2):
                a = own[h][0]
                left = jnp.concatenate([tabs[h, pl.ds(pl.multiple_of(ROWS * p + k * YC, YC), YC)] for p in range(4)], 0)
                for n in range(4):
                    lanes = slice(256 * n, 256 * n + 256)
                    out = lax.dot_general(left, m2[h, lanes], (((1,), (1,)), ((), ())), preferred_element_type=F32)
                    s4[h, :, rows, lanes] = out.reshape(4, YC, 256).astype(BF)
                for d in range(1, 4):
                    four(h, d, k).start()
                back[h, a, rows] = s4[h, a, rows]

        @pl.when(it < ITERS - 1)
        def _():
            @pl.loop(0, chunks)
            def _(k):
                for h in range(2):
                    for d in range(1, 4):
                        four(h, d, k).wait()
                update(k)

                @pl.when(it == ITERS - 2)
                def _():
                    pltpu.make_async_copy(state.at[:, rows_of(k)], state_out.at[:, rows_of(k)], lsem.at[1 + k]).start()

                forward(k, lambda c, rows: state[c, rows])

    for k in range(chunks):
        for h in range(2):
            for d in range(1, 4):
                four(h, d, k).wait()
        pltpu.make_async_copy(back.at[:, :, rows_of(k)], back_out.at[:, :, rows_of(k)], lsem.at[4 + k]).start()
    for k in range(chunks):
        pltpu.make_async_copy(state.at[:, rows_of(k)], state_out.at[:, rows_of(k)], lsem.at[1 + k]).wait()
        pltpu.make_async_copy(back.at[:, :, rows_of(k)], back_out.at[:, :, rows_of(k)], lsem.at[4 + k]).wait()


def steps(forcing, weights, ytab, fwd, inv, pick, wt, cols, bias):
    near_shape = (2, 4, ROWS, NX)
    chunks = ROWS // YC
    any_space = pl.BlockSpec(memory_space=pl.ANY)
    vmem = pl.BlockSpec(memory_space=pltpu.VMEM)
    dma = pltpu.SemaphoreType.DMA
    return pl.pallas_call(
        steps_body, name="steps",
        in_specs=[any_space] * 5 + [vmem] * 3 + [SMEM],
        out_specs=[any_space, any_space],
        out_shape=[jax.ShapeDtypeStruct((C, ROWS, NX), BF), jax.ShapeDtypeStruct(near_shape, BF)],
        scratch_shapes=[
            pltpu.VMEM((C, ROWS, NX), BF),
            pltpu.VMEM((C, ROWS, NX), BF),
            pltpu.VMEM(fwd.shape, BF),
            pltpu.VMEM(inv.shape, BF),
            pltpu.VMEM((C * 16, C * 16), BF),
            pltpu.VMEM((2, 8, C, C, M), BF),
            pltpu.VMEM((2, 4 * ROWS, 2 * M), BF),
            pltpu.VMEM(near_shape, BF),
            pltpu.VMEM(near_shape, BF),
            pltpu.VMEM((2, 4, 16, 16, M), F32),
            pltpu.VMEM((2, 4, 16, 16, M), BF),
            pltpu.VMEM((2, 3, 16, 16, M), BF),
            pltpu.VMEM((C, 16, M), F32),
            pltpu.VMEM((16 * 16, M), F32),
            pltpu.VMEM((2, 4, 16, 16, M), BF),
            pltpu.VMEM((2, NX, 2 * M), BF),
            pltpu.VMEM(near_shape, BF),
            pltpu.VMEM(near_shape, BF),
            dma((9,)),
            dma((2, 3, chunks)), dma((2, 3, chunks)),
            dma((2, 3)), dma((2, 3)), dma((2, 3)), dma((2, 3)),
            dma((2, 3, chunks)), dma((2, 3, chunks)),
        ],
        compiler_params=pltpu.CompilerParams(collective_id=1, has_side_effects=True, vmem_limit_bytes=LIMIT),
    )(forcing, weights, ytab, fwd, inv, pick, wt, cols, bias)


def shifted(field, step, axis):
    return pltpu.roll(field, step % field.shape[axis], axis)


def diff_x(field):
    return (shifted(field, -1, 1) - shifted(field, 1, 1)) * 0.5


def diff_y(field, before, after):
    at = lax.broadcasted_iota(jnp.int32, field.shape, 0)
    upper = jnp.where(at == field.shape[0] - 1, after, shifted(field, -1, 0))
    lower = jnp.where(at == 0, before, shifted(field, 1, 0))
    return (upper - lower) * 0.5


def tail_body(fields_ref, turning_ref, depth_ref, out_ref, own, other, chip, lower, total, share, up_out, up_in,
              geo, edge_out, edge_in, ss, rs):
    lev = lax.axis_index("lev")
    g = lax.axis_index("gy")
    x, c = lev // 2, lev % 2
    partner = {"lev": 2 * x + 1 - c}
    next_row, last_row = {"gy": (g + 1) % 16}, {"gy": (g + 15) % 16}
    beside = {"lev": (lev + 1 + 6 * (1 - c)) % 8}
    barrier = pltpu.get_barrier_semaphore()
    for peer in [partner, beside, next_row, last_row] + [{"lev": (lev + 2 * d) % 8} for d in range(1, 4)]:
        pl.semaphore_signal(barrier, 1, device_id=peer, device_id_type=MESH)

    def copy(src, dst, at, peer):
        return pltpu.make_async_remote_copy(src_ref=src, dst_ref=dst, send_sem=ss.at[at], recv_sem=rs.at[at],
                                            device_id=peer, device_id_type=MESH)

    half = pl.ds(pl.multiple_of(48 * c, 48), 48)
    rest = pl.ds(pl.multiple_of(48 * (1 - c), 48), 48)
    weighted = fields_ref[3] * depth_ref[lev]
    own[...] = weighted.astype(BF)
    up_out[...] = fields_ref[2].astype(BF)
    edge_out[0] = fields_ref[1, 88:96]
    edge_out[1] = fields_ref[1, 0:8]
    pl.semaphore_wait(barrier, 7)
    all_rows = copy(own, other, 0, partner)
    some_rows = copy(own.at[0:48], other.at[0:48], 0, partner)

    @pl.when(c == 0)
    def _():
        all_rows.start()

    @pl.when(c == 1)
    def _():
        some_rows.start()

    winds = [copy(edge_out.at[0], edge_in.at[0], 1, next_row), copy(edge_out.at[1], edge_in.at[1], 2, last_row)]
    for w in winds:
        w.start()

    @pl.when(c == 0)
    def _():
        all_rows.wait_send()
        some_rows.wait_recv()

    @pl.when(c == 1)
    def _():
        some_rows.wait_send()
        all_rows.wait_recv()

    chip[...] = (own[half, :].astype(F32) + other[half, :].astype(F32)).astype(BF)
    sums = [copy(chip, lower.at[d - 1], 2 + d, {"lev": (lev + 2 * d) % 8}) for d in range(1, 4)]
    for d in range(1, 4):
        @pl.when(x + d <= 3)
        def _():
            sums[d - 1].start()

    rising = copy(up_out, up_in, 6, {"lev": (lev + 1) % 8})

    @pl.when(lev < 7)
    def _():
        rising.start()

    for w in winds:
        w.wait()
    east, north = fields_ref[0], fields_ref[1]
    out_ref[0] = diff_x(east) + diff_y(north, edge_in[0, 7:8], edge_in[1, 0:1]) + fields_ref[2]
    total[half, :] = jnp.zeros((48, NX), F32)
    for d in range(1, 4):
        @pl.when(x >= d)
        def _():
            sums[d - 1].wait_recv()
            total[half, :] += lower[d - 1].astype(F32)

    share[...] = total[half, :]
    shared = copy(share, total.at[half], 7, partner)
    shared.start()

    @pl.when(lev >= 1)
    def _():
        rising.wait_recv()
        out_ref[0] -= up_in[...].astype(F32)

    shared.wait()
    geo[...] = total[...] + fields_ref[3] * depth_ref[lev]

    @pl.when(c == 1)
    def _():
        geo[...] += other[...].astype(F32)

    edges = [copy(geo.at[88:96], edge_in.at[2], 8, next_row), copy(geo.at[0:8], edge_in.at[3], 9, last_row)]
    for e in edges:
        e.start()
    out_ref[1] = turning_ref[...] * north - diff_x(geo[...])
    for e in edges:
        e.wait()
    out_ref[2] = turning_ref[...] * east + diff_y(geo[...], edge_in[2, 7:8], edge_in[3, 0:1])
    for d in range(1, 4):
        @pl.when(x + d <= 3)
        def _():
            sums[d - 1].wait_send()

    @pl.when(lev < 7)
    def _():
        rising.wait_send()


def tail_step(fields, coriolis, layer_depth):
    vmem = pl.BlockSpec(memory_space=pltpu.VMEM)
    rows = (ROWS, NX)
    return pl.pallas_call(
        tail_body, name="tail_step", in_specs=[vmem, vmem, SMEM], out_specs=vmem,
        out_shape=jax.ShapeDtypeStruct((3, *rows), F32),
        scratch_shapes=[
            pltpu.VMEM(rows, BF), pltpu.VMEM(rows, BF), pltpu.VMEM((48, NX), BF), pltpu.VMEM((3, 48, NX), BF),
            pltpu.VMEM(rows, F32), pltpu.VMEM((48, NX), F32), pltpu.VMEM(rows, BF), pltpu.VMEM(rows, BF),
            pltpu.VMEM(rows, F32), pltpu.VMEM((2, 8, NX), F32), pltpu.VMEM((4, 8, NX), F32),
            pltpu.SemaphoreType.DMA((10,)), pltpu.SemaphoreType.DMA((10,)),
        ],
        compiler_params=pltpu.CompilerParams(collective_id=2, has_side_effects=True, vmem_limit_bytes=24 << 20),
    )(fields, coriolis[:, None], layer_depth)


@functools.lru_cache(None)
def kron_parts():
    order = np.arange(C).reshape(2, 8, 2).transpose(0, 2, 1).reshape(C)
    pick = np.zeros((C, C), np.float32)
    pick[np.arange(C), order] = 1.0
    spread = np.repeat(np.eye(C, dtype=np.float32), 16, 1)
    four = np.repeat(np.eye(4, dtype=np.float32), 16, 0)
    return [v.astype(BF) for v in (np.repeat(pick, 16, 0), spread, four, pick.T @ spread)]


def on_device(forcing, spectral_weight, point_weight, point_bias, decoder, coriolis, layer_depth):
    source = forcing[0]
    fwd, inv = (jnp.asarray(v) for v in x_tables())
    ytab = jnp.asarray(y_tables())
    pick, cols, four, dec_cols = [jnp.asarray(v) for v in kron_parts()]
    wt = point_weight.T
    state, back = steps(source, spectral_weight, ytab, fwd, inv, pick, wt, cols, point_bias)
    final, fields = last_local(back, state, source, pick, wt, cols, point_bias, four, decoder, dec_cols, inv)
    residual = tail_step(fields, coriolis, layer_depth)
    return final[None], residual[:, None]


def solution(mesh):
    return jax.shard_map(
        on_device,
        mesh=mesh,
        in_specs=(
            P("lev", None, "gy", None),
            P(None, "gy", None, None, None),
            P(),
            P(),
            P(),
            P("gy"),
            P(),
        ),
        out_specs=(P("lev", None, "gy", None), P(None, "lev", "gy", None)),
        check_vma=False,
    )
```

```python
import functools
import math

import jax
import jax.numpy as jnp
import numpy as np
from jax import lax
from jax.experimental import pallas as pl
from jax.experimental.pallas import tpu as pltpu
from jax.sharding import PartitionSpec as P

C = 32
NX = 1024
NY = 1536
M = 128
ROWS = 96
ITERS = 3
MESH = pl.DeviceIdType.MESH
BF = jnp.bfloat16
F32 = jnp.float32
YC = 32
LC = 16
TILE = 256


def turns(a, b, length):
    phase = (a[:, None] * b[None, :]) % length
    return phase.astype(np.float32) * np.float32(2.0 * math.pi / length)


def lane_modes(half, order):
    p, r, s, j = np.meshgrid(np.array(order), np.arange(2), np.arange(4), np.arange(8), indexing="ij")
    k = 32 * s + 8 * p + j if half == 0 else 32 * p + 8 * s + j
    return k.reshape(-1), r.reshape(-1)


@functools.lru_cache(None)
def x_tables():
    forward, inverse = [], []
    for half in range(2):
        for order in ((0, 1, 2, 3), (1, 0, 3, 2)):
            k, r = lane_modes(half, order)
            turned = turns(np.arange(NX), k, NX)
            wave = np.where(r == 0, np.cos(turned), -np.sin(turned)).astype(np.float32)
            factor = np.where(k == 0, 1.0, 2.0).astype(np.float32) / np.float32(NX * NY)
            forward.append(wave)
            inverse.append((wave * factor[None, :]).T)
    return np.stack(forward).astype(BF), np.stack(inverse).astype(BF)


@functools.lru_cache(None)
def y_tables():
    m = np.arange(M)
    signed = np.where(m < M // 2, m, m + NY - M)
    rows = np.arange(NY)
    turned = turns(rows, signed, NY)
    both = np.concatenate([np.cos(turned), np.sin(turned)], 1).astype(np.float32).astype(BF)
    blocks = both.reshape(4, 4, ROWS, 2 * M)
    first = blocks.reshape(4, 4 * ROWS, 2 * M)
    second = blocks.transpose(1, 0, 2, 3).reshape(4, 4 * ROWS, 2 * M)
    return np.stack([first, second])


def gelu(v):
    inner = v * (math.sqrt(2.0 / math.pi) + (math.sqrt(2.0 / math.pi) * 0.044715) * (v * v))
    return (0.5 * v) * (1.0 + jnp.tanh(inner))


def lane_mask(rows):
    return lax.broadcasted_iota(jnp.int32, (rows, 128), 1) < 64


SMEM = pl.BlockSpec(memory_space=pltpu.SMEM)
LIMIT = 42 << 20


def shifted(field, step, axis):
    return pltpu.roll(field, step % field.shape[axis], axis)


def diff_x(field):
    return (shifted(field, -1, 1) - shifted(field, 1, 1)) * 0.5


def diff_y(field, before, after):
    at = lax.broadcasted_iota(jnp.int32, field.shape, 0)
    upper = jnp.where(at == field.shape[0] - 1, after, shifted(field, -1, 0))
    lower = jnp.where(at == 0, before, shifted(field, 1, 0))
    return (upper - lower) * 0.5


def tail_peers():
    lev = lax.axis_index("lev")
    g = lax.axis_index("gy")
    x, c = lev // 2, lev % 2
    beside = {"lev": (lev + 1 + 6 * (1 - c)) % 8}
    near_by = [{"lev": 2 * x + 1 - c}, beside, {"gy": (g + 1) % 16}, {"gy": (g + 15) % 16}]
    return near_by + [{"lev": (lev + 2 * d) % 8} for d in range(1, 4)]


def tail_body(fields_ref, turning_ref, depth_ref, out_ref, own, other, chip, lower, total, share, up_out, up_in,
              geo, edge_out, edge_in, ss, rs):
    lev = lax.axis_index("lev")
    g = lax.axis_index("gy")
    x, c = lev // 2, lev % 2
    partner = {"lev": 2 * x + 1 - c}
    next_row, last_row = {"gy": (g + 1) % 16}, {"gy": (g + 15) % 16}

    def copy(src, dst, at, peer):
        return pltpu.make_async_remote_copy(src_ref=src, dst_ref=dst, send_sem=ss.at[at], recv_sem=rs.at[at],
                                            device_id=peer, device_id_type=MESH)

    spot = lax.broadcasted_iota(jnp.int32, (ROWS, ROWS), 0) == lax.broadcasted_iota(jnp.int32, (ROWS, ROWS), 1)
    turning = jnp.sum(jnp.where(spot, jnp.broadcast_to(turning_ref[...], (ROWS, ROWS)), 0.0), 1, keepdims=True)
    half = pl.ds(pl.multiple_of(48 * c, 48), 48)
    rest = pl.ds(pl.multiple_of(48 * (1 - c), 48), 48)
    weighted = fields_ref[3] * depth_ref[lev]
    own[...] = weighted.astype(BF)
    up_out[...] = fields_ref[2].astype(BF)
    edge_out[0] = fields_ref[1, 88:96]
    edge_out[1] = fields_ref[1, 0:8]
    all_rows = copy(own, other, 0, partner)
    some_rows = copy(own.at[0:48], other.at[0:48], 0, partner)

    @pl.when(c == 0)
    def _():
        all_rows.start()

    @pl.when(c == 1)
    def _():
        some_rows.start()

    winds = [copy(edge_out.at[0], edge_in.at[0], 1, next_row), copy(edge_out.at[1], edge_in.at[1], 2, last_row)]
    for w in winds:
        w.start()

    @pl.when(c == 0)
    def _():
        all_rows.wait_send()
        some_rows.wait_recv()

    @pl.when(c == 1)
    def _():
        some_rows.wait_send()
        all_rows.wait_recv()

    chip[...] = (own[half, :].astype(F32) + other[half, :].astype(F32)).astype(BF)
    sums = [copy(chip, lower.at[d - 1], 2 + d, {"lev": (lev + 2 * d) % 8}) for d in range(1, 4)]
    for d in range(1, 4):
        @pl.when(x + d <= 3)
        def _():
            sums[d - 1].start()

    rising = copy(up_out, up_in, 6, {"lev": (lev + 1) % 8})

    @pl.when(lev < 7)
    def _():
        rising.start()

    for w in winds:
        w.wait()
    east, north = fields_ref[0], fields_ref[1]
    out_ref[0] = diff_x(east) + diff_y(north, edge_in[0, 7:8], edge_in[1, 0:1]) + fields_ref[2]
    total[half, :] = jnp.zeros((48, NX), F32)
    for d in range(1, 4):
        @pl.when(x >= d)
        def _():
            sums[d - 1].wait_recv()
            total[half, :] += lower[d - 1].astype(F32)

    share[...] = total[half, :]
    shared = copy(share, total.at[half], 7, partner)
    shared.start()

    @pl.when(lev >= 1)
    def _():
        rising.wait_recv()
        out_ref[0] -= up_in[...].astype(F32)

    shared.wait()
    geo[...] = total[...] + fields_ref[3] * depth_ref[lev]

    @pl.when(c == 1)
    def _():
        geo[...] += other[...].astype(F32)

    edges = [copy(geo.at[88:96], edge_in.at[2], 8, next_row), copy(geo.at[0:8], edge_in.at[3], 9, last_row)]
    for e in edges:
        e.start()
    out_ref[1] = turning * north - diff_x(geo[...])
    for e in edges:
        e.wait()
    out_ref[2] = turning * east + diff_y(geo[...], edge_in[2, 7:8], edge_in[3, 0:1])
    for d in range(1, 4):
        @pl.when(x + d <= 3)
        def _():
            sums[d - 1].wait_send()

    @pl.when(lev < 7)
    def _():
        rising.wait_send()


def dot_last(left, right):
    return lax.dot_general(left, right, (((1,), (1,)), ((), ())), preferred_element_type=F32)


def kron_values(left, cols):
    left = left.astype(BF)
    full = jnp.dot(left, cols, preferred_element_type=F32)
    i = lax.broadcasted_iota(jnp.int32, full.shape, 0) % 16
    j = lax.broadcasted_iota(jnp.int32, full.shape, 1) % 16
    return jnp.where(i == j, full, 0.0).astype(BF)


def steps_body(forcing_ref, weight_ref, ytab_ref, fwd_hbm, inv_hbm, pick_ref, wt_ref, cols_ref, four_ref, dec_ref,
               dcols_ref, turning_ref, bias_ref, depth_ref, final, out_ref,
               source, state, fwd, inv, kron, wbuf, tabs, near, r1, part, s2, r2, sp, mx, acc, r3, m2, s4, back,
               dmat, hold, fields, own_heat, other_heat, chip, lower, total, share, up_out, up_in, geo,
               edge_out, edge_in, ts, tr, lsem, s1s, s1r, s2s, s2r, s3s, s3r, s4s, s4r):
    g = lax.axis_index("gy")
    z, y = g // 4, g % 4
    own = ((y, z), (z, y))

    def first_peer(h, a):
        return {"gy": z * 4 + a} if h == 0 else {"gy": a * 4 + y}

    def second_peer(h, b):
        return {"gy": b * 4 + y} if h == 0 else {"gy": z * 4 + b}

    barrier = pltpu.get_barrier_semaphore()
    for h in range(2):
        for d in range(1, 4):
            pl.semaphore_signal(barrier, 1, device_id=first_peer(h, (own[h][0] + d) % 4), device_id_type=MESH)

    for peer in tail_peers():
        pl.semaphore_signal(barrier, 1, device_id=peer, device_id_type=MESH)

    def rows_of(k):
        return pl.ds(pl.multiple_of(k * YC, YC), YC)

    def few_of(k):
        return pl.ds(pl.multiple_of(k * LC, LC), LC)

    chunks = ROWS // YC
    pieces = ROWS // LC
    early = 64 // LC

    def local(src, dst, at):
        return pltpu.make_async_copy(src, dst, lsem.at[at])

    load_fwd = local(fwd_hbm, fwd, 0)
    load_source = [local(forcing_ref.at[:, rows_of(k)], source.at[:, rows_of(k)], 1 + k) for k in range(chunks)]
    load_tabs = [local(ytab_ref.at[h, own[h][1]], tabs.at[h], 4 + h) for h in range(2)]
    load_weights = local(weight_ref, wbuf, 6)
    load_inv = local(inv_hbm, inv, 7)
    load_state = local(forcing_ref, state, 8)
    for c in [load_fwd, *load_source, *load_tabs, load_weights, load_inv, load_state]:
        c.start()

    def remote(src, dst, send, recv, peer):
        return pltpu.make_async_remote_copy(src_ref=src, dst_ref=dst, send_sem=send, recv_sem=recv, device_id=peer,
                                            device_id_type=MESH)

    def one(h, d, k):
        a = own[h][0]
        return remote(near.at[h, (a + d) % 4, few_of(k)], r1.at[h, a, few_of(k)], s1s.at[h, d - 1, k],
                      s1r.at[h, d - 1, k], first_peer(h, (a + d) % 4))

    def two(h, d):
        b = own[h][1]
        return remote(s2.at[h, (b + d) % 4], r2.at[h, d - 1], s2s.at[h, d - 1], s2r.at[h, d - 1],
                      second_peer(h, (b + d) % 4))

    def three(h, d):
        b = own[h][1]
        return remote(r3.at[h, b], r3.at[h, b], s3s.at[h, d - 1], s3r.at[h, d - 1], second_peer(h, (b + d) % 4))

    def four(h, d, k):
        a = own[h][0]
        return remote(s4.at[h, (a + d) % 4, rows_of(k)], back.at[h, a, rows_of(k)], s4s.at[h, d - 1, k],
                      s4r.at[h, d - 1, k], first_peer(h, (a + d) % 4))

    def forward(k, load):
        rows = few_of(k)
        mask = lane_mask(LC)
        for h in range(2):
            outs = []
            for par in range(2):
                lhs = jnp.concatenate([load(16 * h + 2 * pair + par, rows) for pair in range(8)], 0)
                outs.append(jnp.dot(lhs, fwd[2 * h + par], preferred_element_type=F32))
            even, odd = outs
            for pair in range(8):
                at = slice(pair * LC, (pair + 1) * LC)
                for v in range(2):
                    e = even[at, 128 * v:128 * v + 128]
                    o = odd[at, 128 * v:128 * v + 128]
                    lanes = slice(128 * pair, 128 * pair + 128)
                    near[h, 2 * v, rows, lanes] = jnp.where(mask, e, o).astype(BF)
                    near[h, 2 * v + 1, rows, lanes] = jnp.where(mask, o, e).astype(BF)
            for d in range(1, 4):
                one(h, d, k).start()
            a = own[h][0]
            r1[h, a, rows] = near[h, a, rows]

    def update(k, sink):
        rows = few_of(k)
        mask = lane_mask(LC)
        groups = []
        for h in range(2):
            even, odd = [], []
            for pair in range(8):
                b = [back[h, p, rows, 128 * pair:128 * pair + 128] for p in range(4)]
                even.append(jnp.concatenate([jnp.where(mask, b[0], b[1]), jnp.where(mask, b[2], b[3])], 1))
                odd.append(jnp.concatenate([jnp.where(mask, b[1], b[0]), jnp.where(mask, b[3], b[2])], 1))
            groups.append(jnp.concatenate(even, 0))
            groups.append(jnp.concatenate(odd, 0))
        for t in range(NX // TILE):
            cols = slice(t * TILE, (t + 1) * TILE)
            mixed = []
            for s in range(LC // 16):
                at = pl.ds(pl.multiple_of(k * LC + 16 * s, 16), 16)
                st = state[:, at, cols].reshape(C * 16, TILE)
                mixed.append(jnp.dot(kron[...], st, preferred_element_type=F32).reshape(4, 8, 16, TILE))
            for q in range(4):
                h, par = q // 2, q % 2
                spread = jnp.dot(groups[q], inv[q, :, cols], preferred_element_type=F32)
                spread = spread.reshape(8, LC, TILE)
                for pair in range(8):
                    c = 16 * h + 2 * pair + par
                    pw = jnp.concatenate([m[q, pair] for m in mixed], 0)
                    v = spread[pair] + pw + (source[c, rows, cols].astype(F32) + bias_ref[c])
                    sink(q, pair, c, rows, cols, gelu(v))

    def keep_state(q, pair, c, rows, cols, value):
        state[c, rows, cols] = value.astype(BF)

    def keep_final(q, pair, c, rows, cols, value):
        final[c, rows, cols] = value
        hold[8 * q + pair, :, cols] = value.astype(BF)

    pl.semaphore_wait(barrier, 13)
    load_fwd.wait()

    @pl.loop(0, chunks)
    def _(k):
        pltpu.make_async_copy(forcing_ref.at[:, rows_of(k)], source.at[:, rows_of(k)], lsem.at[1 + k]).wait()
        pl.loop(0, YC // LC)(lambda t: forward(k * (YC // LC) + t, lambda c, rows: source[c, rows]))

    kron[...] = kron_values(dot_last(pick_ref[...], wt_ref[...]), cols_ref[...])
    dmat[...] = kron_values(jnp.dot(four_ref[...], dec_ref[...], preferred_element_type=F32), dcols_ref[...])
    for c in [*load_tabs, load_weights, load_inv, load_state]:
        c.wait()

    @pl.loop(0, ITERS)
    def _(it):
        for h in range(2):
            for k in range(early):
                for d in range(1, 4):
                    one(h, d, k).wait()

            @pl.loop(0, 4)
            def _(n):
                cols = pl.ds(pl.multiple_of(n * 256, 256), 256)
                x = r1[h, :, 0:64, cols].reshape(256, 256)
                table = tabs[h].reshape(4, ROWS, 2 * M)[:, 0:64].reshape(256, 2 * M)
                acc[h, n] = lax.dot_general(x, table, (((0,), (0,)), ((), ())), preferred_element_type=F32)

        for h in range(2):
            a, b = own[h]
            for k in range(early, pieces):
                for d in range(1, 4):
                    one(h, d, k).wait()

            @pl.loop(0, 4)
            def _(n):
                cols = pl.ds(pl.multiple_of(n * 256, 256), 256)
                x = r1[h, :, 64:96, cols].reshape(128, 256)
                table = tabs[h].reshape(4, ROWS, 2 * M)[:, 64:96].reshape(128, 2 * M)
                pt = acc[h, n] + lax.dot_general(x, table, (((0,), (0,)), ((), ())), preferred_element_type=F32)
                pt = pt.reshape(2, 2, 2, 4, 8, 256)
                for pair in range(2):
                    for h2 in range(2):
                        q0, q1 = pt[pair, h2, 0], pt[pair, h2, 1]
                        re = q0[..., :M] + q1[..., M:]
                        im = q1[..., :M] - q0[..., M:]
                        both = jnp.concatenate([re, im], 1)
                        c = 2 * (2 * n + pair) + lax.rem(h2 + a, 2)
                        part[h, :, c] = both
                        s2[h, :, c] = both.astype(BF)

            for d in range(1, 4):
                two(h, d).start()
        for h in range(2):
            b = own[h][1]
            for d in range(1, 4):
                two(h, d).wait()

            @pl.loop(0, 16)
            def _(c):
                total = part[h, b, c]
                for d in range(3):
                    total = total + r2[h, d, c].astype(F32)
                sp[16 * h + c] = total

            for oh in range(2):
                outs = pl.ds(16 * oh, 16)
                for j in range(8):
                    def add(i, acc):
                        ar, ai = acc
                        wr = wbuf[0, j, i, outs].astype(F32)
                        wi = wbuf[1, j, i, outs].astype(F32)
                        sr = jnp.broadcast_to(sp[i, pl.ds(j, 1), :], (16, M))
                        si = jnp.broadcast_to(sp[i, pl.ds(8 + j, 1), :], (16, M))
                        return ar + (sr * wr - si * wi), ai + (sr * wi + si * wr)

                    re_at, im_at = pl.ds(j, 16, stride=16), pl.ds(8 + j, 16, stride=16)
                    if h == 0:
                        begin = (jnp.zeros((16, M), F32), jnp.zeros((16, M), F32))
                    else:
                        begin = (mx[oh, re_at, :], mx[oh, im_at, :])
                    ar, ai = lax.fori_loop(16 * h, 16 * h + 16, add, begin, unroll=8)
                    mx[oh, re_at, :] = ar
                    mx[oh, im_at, :] = ai
                if h == 1:
                    r3[oh, own[oh][1]] = mx[oh].reshape(16, 16, M).astype(BF)
                    for d in range(1, 4):
                        three(oh, d).start()

        def back_chunk(h, k):
            rows = rows_of(k)
            a = own[h][0]
            left = jnp.concatenate([tabs[h, pl.ds(pl.multiple_of(ROWS * p + k * YC, YC), YC)] for p in range(4)], 0)
            for n in range(4):
                lanes = slice(256 * n, 256 * n + 256)
                out = lax.dot_general(left, m2[h, lanes], (((1,), (1,)), ((), ())), preferred_element_type=F32)
                s4[h, :, rows, lanes] = out.reshape(4, YC, 256).astype(BF)
            for d in range(1, 4):
                four(h, d, k).start()
            back[h, a, rows] = s4[h, a, rows]

        for h in range(2):
            a = own[h][0]
            for d in range(1, 4):
                three(h, d).wait()

            @pl.loop(0, 8)
            def _(n):
                rows = []
                for h2 in range(2):
                    c = 2 * n + lax.rem(h2 + a, 2)
                    block = r3[h, :, c].astype(F32).reshape(4, 2, 8, M)
                    re = block[:, 0].reshape(32, M)
                    im = block[:, 1].reshape(32, M)
                    rows.append(jnp.concatenate([re, -im], 1))
                    rows.append(jnp.concatenate([im, re], 1))
                m2[h, pl.ds(pl.multiple_of(n * 128, 128), 128)] = jnp.concatenate(rows, 0).astype(BF)

            back_chunk(h, 0)

        @pl.loop(1, chunks)
        def _(k):
            for h in range(2):
                back_chunk(h, k)

        @pl.when(it < ITERS - 1)
        def _():
            @pl.loop(0, chunks)
            def _(k):
                for h in range(2):
                    for d in range(1, 4):
                        four(h, d, k).wait()

                @pl.loop(0, YC // LC)
                def _(t):
                    update(k * (YC // LC) + t, keep_state)
                    forward(k * (YC // LC) + t, lambda c, rows: state[c, rows])

    @pl.loop(0, chunks)
    def _(k):
        for h in range(2):
            for d in range(1, 4):
                four(h, d, k).wait()

        @pl.loop(0, YC // LC)
        def _(t):
            piece = k * (YC // LC) + t
            rows = few_of(piece)
            update(piece, keep_final)
            for s in range(LC // 16):
                part_rows = pl.ds(pl.multiple_of(piece * LC + 16 * s, 16), 16)
                lhs = hold[:, 16 * s:16 * s + 16, :].reshape(C * 16, NX)
                f = jnp.dot(dmat[...], lhs, preferred_element_type=F32)
                fields[:, part_rows, :] = f.reshape(4, 16, NX)

    tail_body(fields, turning_ref, depth_ref, out_ref, own_heat, other_heat, chip, lower, total, share, up_out, up_in,
              geo, edge_out, edge_in, ts, tr)


def steps(forcing, weights, ytab, fwd, inv, pick, wt, cols, four, dec, dcols, turning, bias, depth):
    near_shape = (2, 4, ROWS, NX)
    chunks = ROWS // YC
    flat = (ROWS, NX)
    any_space = pl.BlockSpec(memory_space=pl.ANY)
    vmem = pl.BlockSpec(memory_space=pltpu.VMEM)
    dma = pltpu.SemaphoreType.DMA
    return pl.pallas_call(
        steps_body, name="steps",
        in_specs=[any_space] * 5 + [vmem] * 7 + [SMEM] * 2,
        out_specs=[vmem, vmem],
        out_shape=[pltpu.VMEM((C, ROWS, NX), F32), pltpu.VMEM((3, ROWS, NX), F32)],
        scratch_shapes=[
            pltpu.VMEM((C, ROWS, NX), BF),
            pltpu.VMEM((C, ROWS, NX), BF),
            pltpu.VMEM(fwd.shape, BF),
            pltpu.VMEM(inv.shape, BF),
            pltpu.VMEM((C * 16, C * 16), BF),
            pltpu.VMEM((2, 8, C, C, M), BF),
            pltpu.VMEM((2, 4 * ROWS, 2 * M), BF),
            pltpu.VMEM(near_shape, BF),
            pltpu.VMEM(near_shape, BF),
            pltpu.VMEM((2, 4, 16, 16, M), F32),
            pltpu.VMEM((2, 4, 16, 16, M), BF),
            pltpu.VMEM((2, 3, 16, 16, M), BF),
            pltpu.VMEM((C, 16, M), F32),
            pltpu.VMEM((2, 16 * 16, M), F32),
            pltpu.VMEM((2, 4, 256, 256), F32),
            pltpu.VMEM((2, 4, 16, 16, M), BF),
            pltpu.VMEM((2, NX, 2 * M), BF),
            pltpu.VMEM(near_shape, BF),
            pltpu.VMEM(near_shape, BF),
            pltpu.VMEM((64, C * 16), BF), pltpu.VMEM((C, LC, NX), BF),
            pltpu.VMEM((4, ROWS, NX), F32),
            pltpu.VMEM(flat, BF), pltpu.VMEM(flat, BF), pltpu.VMEM((48, NX), BF), pltpu.VMEM((3, 48, NX), BF),
            pltpu.VMEM(flat, F32), pltpu.VMEM((48, NX), F32), pltpu.VMEM(flat, BF), pltpu.VMEM(flat, BF),
            pltpu.VMEM(flat, F32), pltpu.VMEM((2, 8, NX), F32), pltpu.VMEM((4, 8, NX), F32), dma((10,)), dma((10,)),
            dma((9,)),
            dma((2, 3, ROWS // LC)), dma((2, 3, ROWS // LC)),
            dma((2, 3)), dma((2, 3)), dma((2, 3)), dma((2, 3)),
            dma((2, 3, chunks)), dma((2, 3, chunks)),
        ],
        compiler_params=pltpu.CompilerParams(collective_id=1, has_side_effects=True, vmem_limit_bytes=LIMIT),
    )(forcing, weights, ytab, fwd, inv, pick, wt, cols, four, dec, dcols, turning, bias, depth)


def finish_body(final_ref, residual_ref, final_out, residual_out, sem):
    copies = [pltpu.make_async_copy(final_ref.at[pl.ds(4 * i, 4)], final_out.at[pl.ds(4 * i, 4)], sem.at[i]) for i in range(8)]
    copies.append(pltpu.make_async_copy(residual_ref, residual_out, sem.at[8]))
    for c in copies:
        c.start()
    for c in copies:
        c.wait()


def finish(final, residual):
    any_space = pl.BlockSpec(memory_space=pl.ANY)
    return pl.pallas_call(
        finish_body, name="finish", in_specs=[pl.BlockSpec(memory_space=pltpu.VMEM)] * 2, out_specs=[any_space] * 2,
        out_shape=[jax.ShapeDtypeStruct(final.shape, F32), jax.ShapeDtypeStruct(residual.shape, F32)],
        scratch_shapes=[pltpu.SemaphoreType.DMA((9,))],
        compiler_params=pltpu.CompilerParams(vmem_limit_bytes=1 << 20),
    )(final, residual)


@functools.lru_cache(None)
def kron_parts():
    order = np.arange(C).reshape(2, 8, 2).transpose(0, 2, 1).reshape(C)
    pick = np.zeros((C, C), np.float32)
    pick[np.arange(C), order] = 1.0
    spread = np.repeat(np.eye(C, dtype=np.float32), 16, 1)
    four = np.repeat(np.eye(4, dtype=np.float32), 16, 0)
    return [v.astype(BF) for v in (np.repeat(pick, 16, 0), spread, four, pick.T @ spread)]


def on_device(forcing, spectral_weight, point_weight, point_bias, decoder, coriolis, layer_depth):
    source = forcing[0]
    fwd, inv = (jnp.asarray(v) for v in x_tables())
    ytab = jnp.asarray(y_tables())
    pick, cols, four, dec_cols = [jnp.asarray(v) for v in kron_parts()]
    final, residual = steps(source, spectral_weight, ytab, fwd, inv, pick, point_weight, cols, four, decoder, dec_cols,
                            coriolis[None], point_bias, layer_depth)
    final, residual = finish(final, residual)
    return final[None], residual[:, None]


def solution(mesh):
    return jax.shard_map(
        on_device,
        mesh=mesh,
        in_specs=(
            P("lev", None, "gy", None),
            P(None, "gy", None, None, None),
            P(),
            P(),
            P(),
            P("gy"),
            P(),
        ),
        out_specs=(P("lev", None, "gy", None), P(None, "lev", "gy", None)),
        check_vma=False,
    )
```

```python
import functools
import math

import jax
import jax.numpy as jnp
import numpy as np
from jax import lax
from jax.experimental import pallas as pl
from jax.experimental.pallas import tpu as pltpu
from jax.sharding import PartitionSpec as P

C = 32
NX = 1024
NY = 1536
M = 128
ROWS = 96
ITERS = 3
MESH = pl.DeviceIdType.MESH
BF = jnp.bfloat16
F32 = jnp.float32
YC = 32
LC = 32
SPLIT = 3
TILE = 256


def turns(a, b, length):
    phase = (a[:, None] * b[None, :]) % length
    return phase.astype(np.float32) * np.float32(2.0 * math.pi / length)


def lane_modes(half, order):
    p, r, s, j = np.meshgrid(np.array(order), np.arange(2), np.arange(4), np.arange(8), indexing="ij")
    k = 32 * s + 8 * p + j if half == 0 else 32 * p + 8 * s + j
    return k.reshape(-1), r.reshape(-1)


@functools.lru_cache(None)
def x_tables():
    forward, inverse = [], []
    for half in range(2):
        for order in ((0, 1, 2, 3), (1, 0, 3, 2)):
            k, r = lane_modes(half, order)
            turned = turns(np.arange(NX), k, NX)
            wave = np.where(r == 0, np.cos(turned), -np.sin(turned)).astype(np.float32)
            factor = np.where(k == 0, 1.0, 2.0).astype(np.float32) / np.float32(NX * NY)
            forward.append(wave)
            inverse.append((wave * factor[None, :]).T)
    return np.stack(forward).astype(BF), np.stack(inverse).astype(BF)


@functools.lru_cache(None)
def y_tables():
    m = np.arange(M)
    signed = np.where(m < M // 2, m, m + NY - M)
    rows = np.arange(NY)
    turned = turns(rows, signed, NY)
    both = np.concatenate([np.cos(turned), np.sin(turned)], 1).astype(np.float32).astype(BF)
    blocks = both.reshape(4, 4, ROWS, 2 * M)
    first = blocks.reshape(4, 4 * ROWS, 2 * M)
    second = blocks.transpose(1, 0, 2, 3).reshape(4, 4 * ROWS, 2 * M)
    return np.stack([first, second])


def gelu(v):
    inner = v * (math.sqrt(2.0 / math.pi) + (math.sqrt(2.0 / math.pi) * 0.044715) * (v * v))
    return (0.5 * v) * (1.0 + jnp.tanh(inner))


def lane_mask(rows):
    return lax.broadcasted_iota(jnp.int32, (rows, 128), 1) < 64


SMEM = pl.BlockSpec(memory_space=pltpu.SMEM)
LIMIT = 42 << 20


def shifted(field, step, axis):
    return pltpu.roll(field, step % field.shape[axis], axis)


def diff_x(field):
    return (shifted(field, -1, 1) - shifted(field, 1, 1)) * 0.5


def diff_y(field, before, after):
    at = lax.broadcasted_iota(jnp.int32, field.shape, 0)
    upper = jnp.where(at == field.shape[0] - 1, after, shifted(field, -1, 0))
    lower = jnp.where(at == 0, before, shifted(field, 1, 0))
    return (upper - lower) * 0.5


def tail_peers():
    lev = lax.axis_index("lev")
    g = lax.axis_index("gy")
    x, c = lev // 2, lev % 2
    beside = {"lev": (lev + 1 + 6 * (1 - c)) % 8}
    near_by = [{"lev": 2 * x + 1 - c}, beside, {"gy": (g + 1) % 16}, {"gy": (g + 15) % 16}]
    return near_by + [{"lev": (lev + 2 * d) % 8} for d in range(1, 4)]


def tail_body(fields_ref, turning_ref, depth_ref, out_ref, own, other, chip, lower, total, share, up_out, up_in,
              geo, edge_out, edge_in, ss, rs):
    lev = lax.axis_index("lev")
    g = lax.axis_index("gy")
    x, c = lev // 2, lev % 2
    partner = {"lev": 2 * x + 1 - c}
    next_row, last_row = {"gy": (g + 1) % 16}, {"gy": (g + 15) % 16}

    def copy(src, dst, at, peer):
        return pltpu.make_async_remote_copy(src_ref=src, dst_ref=dst, send_sem=ss.at[at], recv_sem=rs.at[at],
                                            device_id=peer, device_id_type=MESH)

    spot = lax.broadcasted_iota(jnp.int32, (ROWS, ROWS), 0) == lax.broadcasted_iota(jnp.int32, (ROWS, ROWS), 1)
    turning = jnp.sum(jnp.where(spot, jnp.broadcast_to(turning_ref[...], (ROWS, ROWS)), 0.0), 1, keepdims=True)
    half = pl.ds(pl.multiple_of(48 * c, 48), 48)
    rest = pl.ds(pl.multiple_of(48 * (1 - c), 48), 48)
    weighted = fields_ref[3] * depth_ref[lev]
    own[...] = weighted.astype(BF)
    up_out[...] = fields_ref[2].astype(BF)
    edge_out[0] = fields_ref[1, 88:96]
    edge_out[1] = fields_ref[1, 0:8]
    all_rows = copy(own, other, 0, partner)
    some_rows = copy(own.at[0:48], other.at[0:48], 0, partner)

    @pl.when(c == 0)
    def _():
        all_rows.start()

    @pl.when(c == 1)
    def _():
        some_rows.start()

    winds = [copy(edge_out.at[0], edge_in.at[0], 1, next_row), copy(edge_out.at[1], edge_in.at[1], 2, last_row)]
    for w in winds:
        w.start()

    @pl.when(c == 0)
    def _():
        all_rows.wait_send()
        some_rows.wait_recv()

    @pl.when(c == 1)
    def _():
        some_rows.wait_send()
        all_rows.wait_recv()

    chip[...] = (own[half, :].astype(F32) + other[half, :].astype(F32)).astype(BF)
    sums = [copy(chip, lower.at[d - 1], 2 + d, {"lev": (lev + 2 * d) % 8}) for d in range(1, 4)]
    for d in range(1, 4):
        @pl.when(x + d <= 3)
        def _():
            sums[d - 1].start()

    rising = copy(up_out, up_in, 6, {"lev": (lev + 1) % 8})

    @pl.when(lev < 7)
    def _():
        rising.start()

    for w in winds:
        w.wait()
    east, north = fields_ref[0], fields_ref[1]
    out_ref[0] = diff_x(east) + diff_y(north, edge_in[0, 7:8], edge_in[1, 0:1]) + fields_ref[2]
    total[half, :] = jnp.zeros((48, NX), F32)
    for d in range(1, 4):
        @pl.when(x >= d)
        def _():
            sums[d - 1].wait_recv()
            total[half, :] += lower[d - 1].astype(F32)

    share[...] = total[half, :]
    shared = copy(share, total.at[half], 7, partner)
    shared.start()

    @pl.when(lev >= 1)
    def _():
        rising.wait_recv()
        out_ref[0] -= up_in[...].astype(F32)

    shared.wait()
    geo[...] = total[...] + fields_ref[3] * depth_ref[lev]

    @pl.when(c == 1)
    def _():
        geo[...] += other[...].astype(F32)

    edges = [copy(geo.at[88:96], edge_in.at[2], 8, next_row), copy(geo.at[0:8], edge_in.at[3], 9, last_row)]
    for e in edges:
        e.start()
    out_ref[1] = turning * north - diff_x(geo[...])
    for e in edges:
        e.wait()
    out_ref[2] = turning * east + diff_y(geo[...], edge_in[2, 7:8], edge_in[3, 0:1])
    for d in range(1, 4):
        @pl.when(x + d <= 3)
        def _():
            sums[d - 1].wait_send()

    @pl.when(lev < 7)
    def _():
        rising.wait_send()


def dot_last(left, right):
    return lax.dot_general(left, right, (((1,), (1,)), ((), ())), preferred_element_type=F32)


def kron_values(left, cols):
    left = left.astype(BF)
    full = jnp.dot(left, cols, preferred_element_type=F32)
    i = lax.broadcasted_iota(jnp.int32, full.shape, 0) % 16
    j = lax.broadcasted_iota(jnp.int32, full.shape, 1) % 16
    return jnp.where(i == j, full, 0.0).astype(BF)


def steps_body(forcing_ref, weight_ref, ytab_ref, fwd_hbm, inv_hbm, pick_ref, wt_ref, cols_ref, four_ref, dec_ref,
               dcols_ref, turning_ref, bias_ref, depth_ref, final, out_ref,
               source, state, fwd, inv, kron, wbuf, tabs, near, r1, part, s2, r2, sp, mx, acc, r3, m2, s4, back,
               dmat, hold, fields, own_heat, other_heat, chip, lower, total, share, up_out, up_in, geo,
               edge_out, edge_in, ts, tr, lsem, s1s, s1r, s2s, s2r, s3s, s3r, s4s, s4r):
    g = lax.axis_index("gy")
    z, y = g // 4, g % 4
    own = ((y, z), (z, y))

    def first_peer(h, a):
        return {"gy": z * 4 + a} if h == 0 else {"gy": a * 4 + y}

    def second_peer(h, b):
        return {"gy": b * 4 + y} if h == 0 else {"gy": z * 4 + b}

    barrier = pltpu.get_barrier_semaphore()
    for h in range(2):
        for d in range(1, 4):
            pl.semaphore_signal(barrier, 1, device_id=first_peer(h, (own[h][0] + d) % 4), device_id_type=MESH)

    for peer in tail_peers():
        pl.semaphore_signal(barrier, 1, device_id=peer, device_id_type=MESH)

    def rows_of(k):
        return pl.ds(pl.multiple_of(k * YC, YC), YC)

    def few_of(k):
        return pl.ds(pl.multiple_of(k * LC, LC), LC)

    chunks = ROWS // YC
    pieces = ROWS // LC
    early = 64 // LC

    def local(src, dst, at):
        return pltpu.make_async_copy(src, dst, lsem.at[at])

    load_fwd = local(fwd_hbm, fwd, 0)
    load_source = [local(forcing_ref.at[:, rows_of(k)], source.at[:, rows_of(k)], 1 + k) for k in range(chunks)]
    load_tabs = [local(ytab_ref.at[h, own[h][1]], tabs.at[h], 4 + h) for h in range(2)]
    load_weights = local(weight_ref, wbuf, 6)
    load_inv = local(inv_hbm, inv, 7)
    load_state = local(forcing_ref, state, 8)
    for c in [load_fwd, *load_source, *load_tabs, load_weights, load_inv, load_state]:
        c.start()

    def remote(src, dst, send, recv, peer):
        return pltpu.make_async_remote_copy(src_ref=src, dst_ref=dst, send_sem=send, recv_sem=recv, device_id=peer,
                                            device_id_type=MESH)

    def one(h, d, k):
        a = own[h][0]
        return remote(near.at[h, (a + d) % 4, few_of(k)], r1.at[h, a, few_of(k)], s1s.at[h, d - 1, k],
                      s1r.at[h, d - 1, k], first_peer(h, (a + d) % 4))

    def two(h, d):
        b = own[h][1]
        return remote(s2.at[h, (b + d) % 4], r2.at[h, d - 1], s2s.at[h, d - 1], s2r.at[h, d - 1],
                      second_peer(h, (b + d) % 4))

    def three(h, d):
        b = own[h][1]
        return remote(r3.at[h, b], r3.at[h, b], s3s.at[h, d - 1], s3r.at[h, d - 1], second_peer(h, (b + d) % 4))

    def four(h, d, k):
        a = own[h][0]
        return remote(s4.at[h, (a + d) % 4, rows_of(k)], back.at[h, a, rows_of(k)], s4s.at[h, d - 1, k],
                      s4r.at[h, d - 1, k], first_peer(h, (a + d) % 4))

    def forward(k, load):
        rows = few_of(k)
        mask = lane_mask(LC)
        for h in range(2):
            outs = []
            for par in range(2):
                lhs = jnp.concatenate([load(16 * h + 2 * pair + par, rows) for pair in range(8)], 0)
                outs.append(jnp.dot(lhs, fwd[2 * h + par], preferred_element_type=F32))
            even, odd = outs
            for pair in range(8):
                at = slice(pair * LC, (pair + 1) * LC)
                for v in range(2):
                    e = even[at, 128 * v:128 * v + 128]
                    o = odd[at, 128 * v:128 * v + 128]
                    lanes = slice(128 * pair, 128 * pair + 128)
                    near[h, 2 * v, rows, lanes] = jnp.where(mask, e, o).astype(BF)
                    near[h, 2 * v + 1, rows, lanes] = jnp.where(mask, o, e).astype(BF)
            for d in range(1, 4):
                one(h, d, k).start()
            a = own[h][0]
            r1[h, a, rows] = near[h, a, rows]

    def update(k, sink):
        rows = few_of(k)
        mask = lane_mask(LC)
        groups = []
        for h in range(2):
            even, odd = [], []
            for pair in range(8):
                b = [back[h, p, rows, 128 * pair:128 * pair + 128] for p in range(4)]
                even.append(jnp.concatenate([jnp.where(mask, b[0], b[1]), jnp.where(mask, b[2], b[3])], 1))
                odd.append(jnp.concatenate([jnp.where(mask, b[1], b[0]), jnp.where(mask, b[3], b[2])], 1))
            groups.append(jnp.concatenate(even, 0))
            groups.append(jnp.concatenate(odd, 0))
        for t in range(NX // TILE):
            cols = slice(t * TILE, (t + 1) * TILE)
            for q in range(4):
                h, par = q // 2, q % 2
                spread = jnp.dot(groups[q], inv[q, :, cols], preferred_element_type=F32)
                spread = spread.reshape(8, LC, TILE)
                for pair in range(8):
                    c = 16 * h + 2 * pair + par
                    sink(q, pair, c, rows, cols, gelu(final[c, rows, cols] + spread[pair]))

    def prepare(first, last):
        @pl.loop(first, last)
        def _(k):
            rows = pl.ds(pl.multiple_of(16 * k, 16), 16)
            for t in range(NX // TILE):
                cols = slice(t * TILE, (t + 1) * TILE)
                st = state[:, rows, cols].reshape(C * 16, TILE)
                mixed = jnp.dot(kron[...], st, preferred_element_type=F32).reshape(4, 8, 16, TILE)
                for q in range(4):
                    for pair in range(8):
                        c = 16 * (q // 2) + 2 * pair + q % 2
                        final[c, rows, cols] = mixed[q, pair] + (source[c, rows, cols].astype(F32) + bias_ref[c])

    def keep_state(q, pair, c, rows, cols, value):
        state[c, rows, cols] = value.astype(BF)

    def keep_final(q, pair, c, rows, cols, value):
        final[c, rows, cols] = value
        hold[8 * q + pair, :, cols] = value.astype(BF)

    pl.semaphore_wait(barrier, 13)
    load_fwd.wait()

    @pl.loop(0, chunks)
    def _(k):
        pltpu.make_async_copy(forcing_ref.at[:, rows_of(k)], source.at[:, rows_of(k)], lsem.at[1 + k]).wait()
        pl.loop(0, YC // LC)(lambda t: forward(k * (YC // LC) + t, lambda c, rows: source[c, rows]))

    kron[...] = kron_values(dot_last(pick_ref[...], wt_ref[...]), cols_ref[...])
    dmat[...] = kron_values(jnp.dot(four_ref[...], dec_ref[...], preferred_element_type=F32), dcols_ref[...])
    for c in [*load_tabs, load_weights, load_inv, load_state]:
        c.wait()

    @pl.loop(0, ITERS)
    def _(it):
        for h in range(2):
            for k in range(early):
                for d in range(1, 4):
                    one(h, d, k).wait()

            @pl.loop(0, 4)
            def _(n):
                cols = pl.ds(pl.multiple_of(n * 256, 256), 256)
                x = r1[h, :, 0:64, cols].reshape(256, 256)
                table = tabs[h].reshape(4, ROWS, 2 * M)[:, 0:64].reshape(256, 2 * M)
                acc[h, n] = lax.dot_general(x, table, (((0,), (0,)), ((), ())), preferred_element_type=F32)

        for h in range(2):
            a, b = own[h]
            for k in range(early, pieces):
                for d in range(1, 4):
                    one(h, d, k).wait()

            @pl.loop(0, 4)
            def _(n):
                cols = pl.ds(pl.multiple_of(n * 256, 256), 256)
                x = r1[h, :, 64:96, cols].reshape(128, 256)
                table = tabs[h].reshape(4, ROWS, 2 * M)[:, 64:96].reshape(128, 2 * M)
                pt = acc[h, n] + lax.dot_general(x, table, (((0,), (0,)), ((), ())), preferred_element_type=F32)
                pt = pt.reshape(2, 2, 2, 4, 8, 256)
                for pair in range(2):
                    for h2 in range(2):
                        q0, q1 = pt[pair, h2, 0], pt[pair, h2, 1]
                        re = q0[..., :M] + q1[..., M:]
                        im = q1[..., :M] - q0[..., M:]
                        both = jnp.concatenate([re, im], 1)
                        c = 2 * (2 * n + pair) + lax.rem(h2 + a, 2)
                        part[h, :, c] = both
                        s2[h, :, c] = both.astype(BF)

            for d in range(1, 4):
                two(h, d).start()

        prepare(0, SPLIT)
        for h in range(2):
            b = own[h][1]
            for d in range(1, 4):
                two(h, d).wait()

            @pl.loop(0, 16)
            def _(c):
                total = part[h, b, c]
                for d in range(3):
                    total = total + r2[h, d, c].astype(F32)
                sp[16 * h + c] = total

            for oh in range(2):
                outs = pl.ds(16 * oh, 16)
                for j in range(8):
                    def add(i, acc):
                        ar, ai = acc
                        wr = wbuf[0, j, i, outs].astype(F32)
                        wi = wbuf[1, j, i, outs].astype(F32)
                        sr = jnp.broadcast_to(sp[i, pl.ds(j, 1), :], (16, M))
                        si = jnp.broadcast_to(sp[i, pl.ds(8 + j, 1), :], (16, M))
                        return ar + (sr * wr - si * wi), ai + (sr * wi + si * wr)

                    re_at, im_at = pl.ds(j, 16, stride=16), pl.ds(8 + j, 16, stride=16)
                    if h == 0:
                        begin = (jnp.zeros((16, M), F32), jnp.zeros((16, M), F32))
                    else:
                        begin = (mx[oh, re_at, :], mx[oh, im_at, :])
                    ar, ai = lax.fori_loop(16 * h, 16 * h + 16, add, begin, unroll=8)
                    mx[oh, re_at, :] = ar
                    mx[oh, im_at, :] = ai
                if h == 1:
                    r3[oh, own[oh][1]] = mx[oh].reshape(16, 16, M).astype(BF)
                    for d in range(1, 4):
                        three(oh, d).start()

        prepare(SPLIT, 6)

        def back_chunk(h, k):
            rows = rows_of(k)
            a = own[h][0]
            left = jnp.concatenate([tabs[h, pl.ds(pl.multiple_of(ROWS * p + k * YC, YC), YC)] for p in range(4)], 0)
            for n in range(4):
                lanes = slice(256 * n, 256 * n + 256)
                out = lax.dot_general(left, m2[h, lanes], (((1,), (1,)), ((), ())), preferred_element_type=F32)
                s4[h, :, rows, lanes] = out.reshape(4, YC, 256).astype(BF)
            for d in range(1, 4):
                four(h, d, k).start()
            back[h, a, rows] = s4[h, a, rows]

        for h in range(2):
            a = own[h][0]
            for d in range(1, 4):
                three(h, d).wait()

            @pl.loop(0, 8)
            def _(n):
                rows = []
                for h2 in range(2):
                    c = 2 * n + lax.rem(h2 + a, 2)
                    block = r3[h, :, c].astype(F32).reshape(4, 2, 8, M)
                    re = block[:, 0].reshape(32, M)
                    im = block[:, 1].reshape(32, M)
                    rows.append(jnp.concatenate([re, -im], 1))
                    rows.append(jnp.concatenate([im, re], 1))
                m2[h, pl.ds(pl.multiple_of(n * 128, 128), 128)] = jnp.concatenate(rows, 0).astype(BF)

            back_chunk(h, 0)

        @pl.loop(1, chunks)
        def _(k):
            for h in range(2):
                back_chunk(h, k)

        @pl.when(it < ITERS - 1)
        def _():
            @pl.loop(0, chunks)
            def _(k):
                for h in range(2):
                    for d in range(1, 4):
                        four(h, d, k).wait()

                @pl.loop(0, YC // LC)
                def _(t):
                    update(k * (YC // LC) + t, keep_state)
                    forward(k * (YC // LC) + t, lambda c, rows: state[c, rows])

    @pl.loop(0, chunks)
    def _(k):
        for h in range(2):
            for d in range(1, 4):
                four(h, d, k).wait()

        @pl.loop(0, YC // LC)
        def _(t):
            piece = k * (YC // LC) + t
            rows = few_of(piece)
            update(piece, keep_final)
            for s in range(LC // 16):
                part_rows = pl.ds(pl.multiple_of(piece * LC + 16 * s, 16), 16)
                lhs = hold[:, 16 * s:16 * s + 16, :].reshape(C * 16, NX)
                f = jnp.dot(dmat[...], lhs, preferred_element_type=F32)
                fields[:, part_rows, :] = f.reshape(4, 16, NX)

    tail_body(fields, turning_ref, depth_ref, out_ref, own_heat, other_heat, chip, lower, total, share, up_out, up_in,
              geo, edge_out, edge_in, ts, tr)


def steps(forcing, weights, ytab, fwd, inv, pick, wt, cols, four, dec, dcols, turning, bias, depth):
    near_shape = (2, 4, ROWS, NX)
    chunks = ROWS // YC
    flat = (ROWS, NX)
    any_space = pl.BlockSpec(memory_space=pl.ANY)
    vmem = pl.BlockSpec(memory_space=pltpu.VMEM)
    dma = pltpu.SemaphoreType.DMA
    return pl.pallas_call(
        steps_body, name="steps",
        in_specs=[any_space] * 5 + [vmem] * 7 + [SMEM] * 2,
        out_specs=[vmem, vmem],
        out_shape=[pltpu.VMEM((C, ROWS, NX), F32), pltpu.VMEM((3, ROWS, NX), F32)],
        scratch_shapes=[
            pltpu.VMEM((C, ROWS, NX), BF),
            pltpu.VMEM((C, ROWS, NX), BF),
            pltpu.VMEM(fwd.shape, BF),
            pltpu.VMEM(inv.shape, BF),
            pltpu.VMEM((C * 16, C * 16), BF),
            pltpu.VMEM((2, 8, C, C, M), BF),
            pltpu.VMEM((2, 4 * ROWS, 2 * M), BF),
            pltpu.VMEM(near_shape, BF),
            pltpu.VMEM(near_shape, BF),
            pltpu.VMEM((2, 4, 16, 16, M), F32),
            pltpu.VMEM((2, 4, 16, 16, M), BF),
            pltpu.VMEM((2, 3, 16, 16, M), BF),
            pltpu.VMEM((C, 16, M), F32),
            pltpu.VMEM((2, 16 * 16, M), F32),
            pltpu.VMEM((2, 4, 256, 256), F32),
            pltpu.VMEM((2, 4, 16, 16, M), BF),
            pltpu.VMEM((2, NX, 2 * M), BF),
            pltpu.VMEM(near_shape, BF),
            pltpu.VMEM(near_shape, BF),
            pltpu.VMEM((64, C * 16), BF), pltpu.VMEM((C, LC, NX), BF),
            pltpu.VMEM((4, ROWS, NX), F32),
            pltpu.VMEM(flat, BF), pltpu.VMEM(flat, BF), pltpu.VMEM((48, NX), BF), pltpu.VMEM((3, 48, NX), BF),
            pltpu.VMEM(flat, F32), pltpu.VMEM((48, NX), F32), pltpu.VMEM(flat, BF), pltpu.VMEM(flat, BF),
            pltpu.VMEM(flat, F32), pltpu.VMEM((2, 8, NX), F32), pltpu.VMEM((4, 8, NX), F32), dma((10,)), dma((10,)),
            dma((9,)),
            dma((2, 3, ROWS // LC)), dma((2, 3, ROWS // LC)),
            dma((2, 3)), dma((2, 3)), dma((2, 3)), dma((2, 3)),
            dma((2, 3, chunks)), dma((2, 3, chunks)),
        ],
        compiler_params=pltpu.CompilerParams(collective_id=1, has_side_effects=True, vmem_limit_bytes=LIMIT),
    )(forcing, weights, ytab, fwd, inv, pick, wt, cols, four, dec, dcols, turning, bias, depth)


def finish_body(final_ref, residual_ref, final_out, residual_out, sem):
    copies = [pltpu.make_async_copy(final_ref.at[pl.ds(4 * i, 4)], final_out.at[pl.ds(4 * i, 4)], sem.at[i]) for i in range(8)]
    copies.append(pltpu.make_async_copy(residual_ref, residual_out, sem.at[8]))
    for c in copies:
        c.start()
    for c in copies:
        c.wait()


def finish(final, residual):
    any_space = pl.BlockSpec(memory_space=pl.ANY)
    return pl.pallas_call(
        finish_body, name="finish", in_specs=[pl.BlockSpec(memory_space=pltpu.VMEM)] * 2, out_specs=[any_space] * 2,
        out_shape=[jax.ShapeDtypeStruct(final.shape, F32), jax.ShapeDtypeStruct(residual.shape, F32)],
        scratch_shapes=[pltpu.SemaphoreType.DMA((9,))],
        compiler_params=pltpu.CompilerParams(vmem_limit_bytes=1 << 20),
    )(final, residual)


@functools.lru_cache(None)
def kron_parts():
    order = np.arange(C).reshape(2, 8, 2).transpose(0, 2, 1).reshape(C)
    pick = np.zeros((C, C), np.float32)
    pick[np.arange(C), order] = 1.0
    spread = np.repeat(np.eye(C, dtype=np.float32), 16, 1)
    four = np.repeat(np.eye(4, dtype=np.float32), 16, 0)
    return [v.astype(BF) for v in (np.repeat(pick, 16, 0), spread, four, pick.T @ spread)]


def on_device(forcing, spectral_weight, point_weight, point_bias, decoder, coriolis, layer_depth):
    source = forcing[0]
    fwd, inv = (jnp.asarray(v) for v in x_tables())
    ytab = jnp.asarray(y_tables())
    pick, cols, four, dec_cols = [jnp.asarray(v) for v in kron_parts()]
    final, residual = steps(source, spectral_weight, ytab, fwd, inv, pick, point_weight, cols, four, decoder, dec_cols,
                            coriolis[None], point_bias, layer_depth)
    final, residual = finish(final, residual)
    return final[None], residual[:, None]


def solution(mesh):
    return jax.shard_map(
        on_device,
        mesh=mesh,
        in_specs=(
            P("lev", None, "gy", None),
            P(None, "gy", None, None, None),
            P(),
            P(),
            P(),
            P("gy"),
            P(),
        ),
        out_specs=(P("lev", None, "gy", None), P(None, "lev", "gy", None)),
        check_vma=False,
    )
```

```python
import functools
import math

import jax
import jax.numpy as jnp
import numpy as np
from jax import lax
from jax.experimental import pallas as pl
from jax.experimental.pallas import tpu as pltpu
from jax.sharding import PartitionSpec as P

C = 32
NX = 1024
NY = 1536
M = 128
ROWS = 96
ITERS = 3
MESH = pl.DeviceIdType.MESH
BF = jnp.bfloat16
F32 = jnp.float32
YC = 32
LC = 32
SPLIT = 3
TILE = 256


def turns(a, b, length):
    phase = (a[:, None] * b[None, :]) % length
    return phase.astype(np.float32) * np.float32(2.0 * math.pi / length)


def lane_modes(half, order):
    p, r, s, j = np.meshgrid(np.array(order), np.arange(2), np.arange(4), np.arange(8), indexing="ij")
    k = 32 * s + 8 * p + j if half == 0 else 32 * p + 8 * s + j
    return k.reshape(-1), r.reshape(-1)


@functools.lru_cache(None)
def x_tables():
    forward, inverse = [], []
    for half in range(2):
        for order in ((0, 1, 2, 3), (1, 0, 3, 2)):
            k, r = lane_modes(half, order)
            turned = turns(np.arange(NX), k, NX)
            wave = np.where(r == 0, np.cos(turned), -np.sin(turned)).astype(np.float32)
            factor = np.where(k == 0, 1.0, 2.0).astype(np.float32) / np.float32(NX * NY)
            forward.append(wave)
            inverse.append((wave * factor[None, :]).T)
    return np.stack(forward).astype(BF), np.stack(inverse).astype(BF)


@functools.lru_cache(None)
def y_tables():
    m = np.arange(M)
    signed = np.where(m < M // 2, m, m + NY - M)
    rows = np.arange(NY)
    turned = turns(rows, signed, NY)
    both = np.concatenate([np.cos(turned), np.sin(turned)], 1).astype(np.float32).astype(BF)
    blocks = both.reshape(4, 4, ROWS, 2 * M)
    first = blocks.reshape(4, 4 * ROWS, 2 * M)
    second = blocks.transpose(1, 0, 2, 3).reshape(4, 4 * ROWS, 2 * M)
    return np.stack([first, second])


def gelu(v):
    inner = v * (math.sqrt(2.0 / math.pi) + (math.sqrt(2.0 / math.pi) * 0.044715) * (v * v))
    return (0.5 * v) * (1.0 + jnp.tanh(inner))


def lane_mask(rows):
    return lax.broadcasted_iota(jnp.int32, (rows, 128), 1) < 64


SMEM = pl.BlockSpec(memory_space=pltpu.SMEM)
LIMIT = 42 << 20


def shifted(field, step, axis):
    return pltpu.roll(field, step % field.shape[axis], axis)


def diff_x(field):
    return (shifted(field, -1, 1) - shifted(field, 1, 1)) * 0.5


def diff_y(field, before, after):
    at = lax.broadcasted_iota(jnp.int32, field.shape, 0)
    upper = jnp.where(at == field.shape[0] - 1, after, shifted(field, -1, 0))
    lower = jnp.where(at == 0, before, shifted(field, 1, 0))
    return (upper - lower) * 0.5


def tail_peers():
    lev = lax.axis_index("lev")
    g = lax.axis_index("gy")
    x, c = lev // 2, lev % 2
    beside = {"lev": (lev + 1 + 6 * (1 - c)) % 8}
    near_by = [{"lev": 2 * x + 1 - c}, beside, {"gy": (g + 1) % 16}, {"gy": (g + 15) % 16}]
    return near_by + [{"lev": (lev + 2 * d) % 8} for d in range(1, 4)]


def tail_body(fields_ref, turning_ref, depth_ref, out_ref, own, other, chip, lower, total, share, up_out, up_in,
              geo, edge_out, edge_in, ss, rs):
    lev = lax.axis_index("lev")
    g = lax.axis_index("gy")
    x, c = lev // 2, lev % 2
    partner = {"lev": 2 * x + 1 - c}
    next_row, last_row = {"gy": (g + 1) % 16}, {"gy": (g + 15) % 16}

    def copy(src, dst, at, peer):
        return pltpu.make_async_remote_copy(src_ref=src, dst_ref=dst, send_sem=ss.at[at], recv_sem=rs.at[at],
                                            device_id=peer, device_id_type=MESH)

    spot = lax.broadcasted_iota(jnp.int32, (ROWS, ROWS), 0) == lax.broadcasted_iota(jnp.int32, (ROWS, ROWS), 1)
    turning = jnp.sum(jnp.where(spot, jnp.broadcast_to(turning_ref[...], (ROWS, ROWS)), 0.0), 1, keepdims=True)
    half = pl.ds(pl.multiple_of(48 * c, 48), 48)
    rest = pl.ds(pl.multiple_of(48 * (1 - c), 48), 48)
    weighted = fields_ref[3] * depth_ref[lev]
    own[...] = weighted.astype(BF)
    up_out[...] = fields_ref[2].astype(BF)
    edge_out[0] = fields_ref[1, 88:96]
    edge_out[1] = fields_ref[1, 0:8]
    all_rows = copy(own, other, 0, partner)
    some_rows = copy(own.at[0:48], other.at[0:48], 0, partner)

    @pl.when(c == 0)
    def _():
        all_rows.start()

    @pl.when(c == 1)
    def _():
        some_rows.start()

    winds = [copy(edge_out.at[0], edge_in.at[0], 1, next_row), copy(edge_out.at[1], edge_in.at[1], 2, last_row)]
    for w in winds:
        w.start()

    @pl.when(c == 0)
    def _():
        all_rows.wait_send()
        some_rows.wait_recv()

    @pl.when(c == 1)
    def _():
        some_rows.wait_send()
        all_rows.wait_recv()

    chip[...] = (own[half, :].astype(F32) + other[half, :].astype(F32)).astype(BF)
    sums = [copy(chip, lower.at[d - 1], 2 + d, {"lev": (lev + 2 * d) % 8}) for d in range(1, 4)]
    for d in range(1, 4):
        @pl.when(x + d <= 3)
        def _():
            sums[d - 1].start()

    rising = copy(up_out, up_in, 6, {"lev": (lev + 1) % 8})

    @pl.when(lev < 7)
    def _():
        rising.start()

    for w in winds:
        w.wait()
    east, north = fields_ref[0], fields_ref[1]
    out_ref[0] = diff_x(east) + diff_y(north, edge_in[0, 7:8], edge_in[1, 0:1]) + fields_ref[2]
    total[half, :] = jnp.zeros((48, NX), F32)
    for d in range(1, 4):
        @pl.when(x >= d)
        def _():
            sums[d - 1].wait_recv()
            total[half, :] += lower[d - 1].astype(F32)

    share[...] = total[half, :]
    shared = copy(share, total.at[half], 7, partner)
    shared.start()

    @pl.when(lev >= 1)
    def _():
        rising.wait_recv()
        out_ref[0] -= up_in[...].astype(F32)

    shared.wait()
    geo[...] = total[...] + fields_ref[3] * depth_ref[lev]

    @pl.when(c == 1)
    def _():
        geo[...] += other[...].astype(F32)

    edges = [copy(geo.at[88:96], edge_in.at[2], 8, next_row), copy(geo.at[0:8], edge_in.at[3], 9, last_row)]
    for e in edges:
        e.start()
    out_ref[1] = turning * north - diff_x(geo[...])
    for e in edges:
        e.wait()
    out_ref[2] = turning * east + diff_y(geo[...], edge_in[2, 7:8], edge_in[3, 0:1])
    for d in range(1, 4):
        @pl.when(x + d <= 3)
        def _():
            sums[d - 1].wait_send()

    @pl.when(lev < 7)
    def _():
        rising.wait_send()


def dot_last(left, right):
    return lax.dot_general(left, right, (((1,), (1,)), ((), ())), preferred_element_type=F32)


def kron_values(left, cols):
    left = left.astype(BF)
    full = jnp.dot(left, cols, preferred_element_type=F32)
    i = lax.broadcasted_iota(jnp.int32, full.shape, 0) % 16
    j = lax.broadcasted_iota(jnp.int32, full.shape, 1) % 16
    return jnp.where(i == j, full, 0.0).astype(BF)


def steps_body(forcing_ref, weight_ref, ytab_ref, fwd_hbm, inv_hbm, pick_ref, wt_ref, cols_ref, four_ref, dec_ref,
               turning_ref, bias_ref, depth_ref, final, out_ref,
               source, state, fwd, inv, kron, wbuf, tabs, near, r1, part, s2, r2, sp, mx, r3, m2, s4, back,
               dmat, fields, own_heat, other_heat, chip, lower, total, share, up_out, up_in, geo,
               edge_out, edge_in, ts, tr, lsem, s1s, s1r, s2s, s2r, s3s, s3r, s4s, s4r):
    g = lax.axis_index("gy")
    z, y = g // 4, g % 4
    own = ((y, z), (z, y))

    def first_peer(h, a):
        return {"gy": z * 4 + a} if h == 0 else {"gy": a * 4 + y}

    def second_peer(h, b):
        return {"gy": b * 4 + y} if h == 0 else {"gy": z * 4 + b}

    barrier = pltpu.get_barrier_semaphore()
    for h in range(2):
        for d in range(1, 4):
            pl.semaphore_signal(barrier, 1, device_id=first_peer(h, (own[h][0] + d) % 4), device_id_type=MESH)

    for peer in tail_peers():
        pl.semaphore_signal(barrier, 1, device_id=peer, device_id_type=MESH)

    def rows_of(k):
        return pl.ds(pl.multiple_of(k * YC, YC), YC)

    def few_of(k):
        return pl.ds(pl.multiple_of(k * LC, LC), LC)

    chunks = ROWS // YC
    pieces = ROWS // LC

    def local(src, dst, at):
        return pltpu.make_async_copy(src, dst, lsem.at[at])

    load_fwd = local(fwd_hbm, fwd, 0)
    load_source = [local(forcing_ref.at[:, rows_of(k)], source.at[:, rows_of(k)], 1 + k) for k in range(chunks)]
    load_tabs = [local(ytab_ref.at[h, own[h][1]], tabs.at[h], 4 + h) for h in range(2)]
    load_weights = local(weight_ref, wbuf, 6)
    load_inv = local(inv_hbm, inv, 7)
    load_state = local(forcing_ref, state, 8)
    for c in [load_fwd, *load_source, *load_tabs, load_weights, load_inv, load_state]:
        c.start()

    def remote(src, dst, send, recv, peer):
        return pltpu.make_async_remote_copy(src_ref=src, dst_ref=dst, send_sem=send, recv_sem=recv, device_id=peer,
                                            device_id_type=MESH)

    def lanes_of(e):
        return slice(512 * e, 512 * e + 512)

    def one(h, d, k, e):
        a = own[h][0]
        return remote(near.at[h, (a + d) % 4, few_of(k), lanes_of(e)], r1.at[h, a, few_of(k), lanes_of(e)],
                      s1s.at[e, h, d - 1, k], s1r.at[e, h, d - 1, k], first_peer(h, (a + d) % 4))

    def two(h, d, e):
        b = own[h][1]
        at = pl.ds(8 * e, 8)
        return remote(s2.at[h, (b + d) % 4, at], r2.at[h, d - 1, at], s2s.at[e, h, d - 1], s2r.at[e, h, d - 1],
                      second_peer(h, (b + d) % 4))

    def three(h, d, e):
        b = own[h][1]
        at = pl.ds(8 * e, 8)
        return remote(r3.at[h, b, at], r3.at[h, b, at], s3s.at[e, h, d - 1], s3r.at[e, h, d - 1],
                      second_peer(h, (b + d) % 4))

    def four(h, d, k, e):
        a = own[h][0]
        return remote(s4.at[h, (a + d) % 4, rows_of(k), lanes_of(e)], back.at[h, a, rows_of(k), lanes_of(e)],
                      s4s.at[e, h, d - 1, k], s4r.at[e, h, d - 1, k], first_peer(h, (a + d) % 4))

    def forward(k, load, e):
        rows = few_of(k)
        mask = lane_mask(LC)
        for h in range(2):
            outs = []
            for par in range(2):
                lhs = jnp.concatenate([load(16 * h + 2 * pair + par, rows) for pair in range(4 * e, 4 * e + 4)], 0)
                outs.append(jnp.dot(lhs, fwd[2 * h + par], preferred_element_type=F32))
            even, odd = outs
            for pair in range(4 * e, 4 * e + 4):
                at = slice((pair - 4 * e) * LC, (pair - 4 * e + 1) * LC)
                for v in range(2):
                    lo = even[at, 128 * v:128 * v + 128]
                    hi = odd[at, 128 * v:128 * v + 128]
                    lanes = slice(128 * pair, 128 * pair + 128)
                    near[h, 2 * v, rows, lanes] = jnp.where(mask, lo, hi).astype(BF)
                    near[h, 2 * v + 1, rows, lanes] = jnp.where(mask, hi, lo).astype(BF)
            for d in range(1, 4):
                one(h, d, k, e).start()
            a = own[h][0]
            r1[h, a, rows, lanes_of(e)] = near[h, a, rows, lanes_of(e)]

    def update(k, sink, e):
        rows = few_of(k)
        mask = lane_mask(LC)
        groups = []
        for h in range(2):
            even, odd = [], []
            for pair in range(4 * e, 4 * e + 4):
                b = [back[h, p, rows, 128 * pair:128 * pair + 128] for p in range(4)]
                even.append(jnp.concatenate([jnp.where(mask, b[0], b[1]), jnp.where(mask, b[2], b[3])], 1))
                odd.append(jnp.concatenate([jnp.where(mask, b[1], b[0]), jnp.where(mask, b[3], b[2])], 1))
            groups.append(jnp.concatenate(even, 0))
            groups.append(jnp.concatenate(odd, 0))
        for t in range(NX // TILE):
            cols = slice(t * TILE, (t + 1) * TILE)
            for q in range(4):
                h, par = q // 2, q % 2
                spread = jnp.dot(groups[q], inv[q, :, cols], preferred_element_type=F32)
                spread = spread.reshape(4, LC, TILE)
                for pair in range(4 * e, 4 * e + 4):
                    c = 16 * h + 2 * pair + par
                    sink(q, pair, c, rows, cols, gelu(final[c, rows, cols] + spread[pair - 4 * e]))

    def prepare(first, last):
        @pl.loop(first, last)
        def _(k):
            rows = pl.ds(pl.multiple_of(16 * k, 16), 16)
            for t in range(NX // TILE):
                cols = slice(t * TILE, (t + 1) * TILE)
                st = state[:, rows, cols].reshape(C * 16, TILE)
                mixed = jnp.dot(kron[...], st, preferred_element_type=F32).reshape(4, 8, 16, TILE)
                for q in range(4):
                    for pair in range(8):
                        c = 16 * (q // 2) + 2 * pair + q % 2
                        final[c, rows, cols] = mixed[q, pair] + (source[c, rows, cols].astype(F32) + bias_ref[c])

    def keep_state(q, pair, c, rows, cols, value):
        state[c, rows, cols] = value.astype(BF)

    def keep_final(q, pair, c, rows, cols, value):
        final[c, rows, cols] = value
        state[c, rows, cols] = value.astype(BF)

    pl.semaphore_wait(barrier, 13)
    load_fwd.wait()

    @pl.loop(0, chunks)
    def _(k):
        pltpu.make_async_copy(forcing_ref.at[:, rows_of(k)], source.at[:, rows_of(k)], lsem.at[1 + k]).wait()
        pl.loop(0, YC // LC)(lambda t: [forward(k * (YC // LC) + t, lambda c, rows: source[c, rows], e) for e in range(2)] and None)

    kron[...] = kron_values(dot_last(pick_ref[...], wt_ref[...]), cols_ref[...])
    dmat[...] = kron_values(jnp.dot(four_ref[...], dec_ref[...], preferred_element_type=F32), cols_ref[...])
    for c in [*load_tabs, load_weights, load_inv, load_state]:
        c.wait()

    @pl.loop(0, ITERS)
    def _(it):
        for e in range(2):
            for h in range(2):
                a = own[h][0]
                for k in range(pieces):
                    for d in range(1, 4):
                        one(h, d, k, e).wait()

                @pl.loop(2 * e, 2 * e + 2)
                def _(n):
                    cols = pl.ds(pl.multiple_of(n * 256, 256), 256)
                    x = r1[h, :, :, cols].reshape(4 * ROWS, 256)
                    pt = lax.dot_general(x, tabs[h], (((0,), (0,)), ((), ())), preferred_element_type=F32)
                    pt = pt.reshape(2, 2, 2, 4, 8, 256)
                    for pair in range(2):
                        for h2 in range(2):
                            q0, q1 = pt[pair, h2, 0], pt[pair, h2, 1]
                            re = q0[..., :M] + q1[..., M:]
                            im = q1[..., :M] - q0[..., M:]
                            both = jnp.concatenate([re, im], 1)
                            c = 2 * (2 * n + pair) + lax.rem(h2 + a, 2)
                            part[h, :, c] = both
                            s2[h, :, c] = both.astype(BF)

                for d in range(1, 4):
                    two(h, d, e).start()

        prepare(0, SPLIT)
        for e, h in ((0, 0), (0, 1), (1, 0), (1, 1)):
            b = own[h][1]
            for d in range(1, 4):
                two(h, d, e).wait()

            @pl.loop(8 * e, 8 * e + 8)
            def _(c):
                total = part[h, b, c]
                for d in range(3):
                    total = total + r2[h, d, c].astype(F32)
                sp[16 * h + c] = total

            for oh in range(2):
                outs = pl.ds(16 * oh, 16)
                for j in range(8):
                    def add(i, acc):
                        ar, ai = acc
                        wr = wbuf[0, j, i, outs].astype(F32)
                        wi = wbuf[1, j, i, outs].astype(F32)
                        sr = jnp.broadcast_to(sp[i, pl.ds(j, 1), :], (16, M))
                        si = jnp.broadcast_to(sp[i, pl.ds(8 + j, 1), :], (16, M))
                        return ar + (sr * wr - si * wi), ai + (sr * wi + si * wr)

                    re_at, im_at = pl.ds(j, 16, stride=16), pl.ds(8 + j, 16, stride=16)
                    if e == 0 and h == 0:
                        begin = (jnp.zeros((16, M), F32), jnp.zeros((16, M), F32))
                    else:
                        begin = (mx[oh, re_at, :], mx[oh, im_at, :])
                    ar, ai = lax.fori_loop(16 * h + 8 * e, 16 * h + 8 * e + 8, add, begin, unroll=8)
                    mx[oh, re_at, :] = ar
                    mx[oh, im_at, :] = ai
                if e == 1 and h == 1:
                    r3[oh, own[oh][1]] = mx[oh].reshape(16, 16, M).astype(BF)
                    for late in range(2):
                        for d in range(1, 4):
                            three(oh, d, late).start()

        prepare(SPLIT, 6)

        def back_chunk(h, k, e):
            rows = rows_of(k)
            a = own[h][0]
            left = jnp.concatenate([tabs[h, pl.ds(pl.multiple_of(ROWS * p + k * YC, YC), YC)] for p in range(4)], 0)
            for n in range(2 * e, 2 * e + 2):
                lanes = slice(256 * n, 256 * n + 256)
                out = lax.dot_general(left, m2[h, lanes], (((1,), (1,)), ((), ())), preferred_element_type=F32)
                s4[h, :, rows, lanes] = out.reshape(4, YC, 256).astype(BF)
            for d in range(1, 4):
                four(h, d, k, e).start()
            back[h, a, rows, lanes_of(e)] = s4[h, a, rows, lanes_of(e)]

        for e in range(2):
            for h in range(2):
                a = own[h][0]
                for d in range(1, 4):
                    three(h, d, e).wait()

                @pl.loop(4 * e, 4 * e + 4)
                def _(n):
                    rows = []
                    for h2 in range(2):
                        c = 2 * n + lax.rem(h2 + a, 2)
                        block = r3[h, :, c].astype(F32).reshape(4, 2, 8, M)
                        re = block[:, 0].reshape(32, M)
                        im = block[:, 1].reshape(32, M)
                        rows.append(jnp.concatenate([re, -im], 1))
                        rows.append(jnp.concatenate([im, re], 1))
                    m2[h, pl.ds(pl.multiple_of(n * 128, 128), 128)] = jnp.concatenate(rows, 0).astype(BF)

                back_chunk(h, 0, e)

            @pl.loop(1, chunks)
            def _(k):
                for h in range(2):
                    back_chunk(h, k, e)

        @pl.when(it < ITERS - 1)
        def _():
            for e in range(2):
                @pl.loop(0, chunks)
                def _(k):
                    for h in range(2):
                        for d in range(1, 4):
                            four(h, d, k, e).wait()
                    update(k, keep_state, e)
                    forward(k, lambda c, rows: state[c, rows], e)

    for e in range(2):
        @pl.loop(0, chunks)
        def _(k):
            for h in range(2):
                for d in range(1, 4):
                    four(h, d, k, e).wait()
            update(k, keep_final, e)
            if e == 1:
                for s in range(YC // 16):
                    rows = pl.ds(pl.multiple_of(k * YC + 16 * s, 16), 16)
                    f = jnp.dot(dmat[...], state[:, rows, :].reshape(C * 16, NX), preferred_element_type=F32)
                    fields[:, rows, :] = f.reshape(4, 16, NX)

    tail_body(fields, turning_ref, depth_ref, out_ref, own_heat, other_heat, chip, lower, total, share, up_out, up_in,
              geo, edge_out, edge_in, ts, tr)


def steps(forcing, weights, ytab, fwd, inv, pick, wt, cols, four, dec, turning, bias, depth):
    near_shape = (2, 4, ROWS, NX)
    chunks = ROWS // YC
    flat = (ROWS, NX)
    any_space = pl.BlockSpec(memory_space=pl.ANY)
    vmem = pl.BlockSpec(memory_space=pltpu.VMEM)
    dma = pltpu.SemaphoreType.DMA
    return pl.pallas_call(
        steps_body, name="steps",
        in_specs=[any_space] * 5 + [vmem] * 6 + [SMEM] * 2,
        out_specs=[vmem, vmem],
        out_shape=[pltpu.VMEM((C, ROWS, NX), F32), pltpu.VMEM((3, ROWS, NX), F32)],
        scratch_shapes=[
            pltpu.VMEM((C, ROWS, NX), BF),
            pltpu.VMEM((C, ROWS, NX), BF),
            pltpu.VMEM(fwd.shape, BF),
            pltpu.VMEM(inv.shape, BF),
            pltpu.VMEM((C * 16, C * 16), BF),
            pltpu.VMEM((2, 8, C, C, M), BF),
            pltpu.VMEM((2, 4 * ROWS, 2 * M), BF),
            pltpu.VMEM(near_shape, BF),
            pltpu.VMEM(near_shape, BF),
            pltpu.VMEM((2, 4, 16, 16, M), F32),
            pltpu.VMEM((2, 4, 16, 16, M), BF),
            pltpu.VMEM((2, 3, 16, 16, M), BF),
            pltpu.VMEM((C, 16, M), F32),
            pltpu.VMEM((2, 16 * 16, M), F32),
            pltpu.VMEM((2, 4, 16, 16, M), BF),
            pltpu.VMEM((2, NX, 2 * M), BF),
            pltpu.VMEM(near_shape, BF),
            pltpu.VMEM(near_shape, BF),
            pltpu.VMEM((64, C * 16), BF),
            pltpu.VMEM((4, ROWS, NX), F32),
            pltpu.VMEM(flat, BF), pltpu.VMEM(flat, BF), pltpu.VMEM((48, NX), BF), pltpu.VMEM((3, 48, NX), BF),
            pltpu.VMEM(flat, F32), pltpu.VMEM((48, NX), F32), pltpu.VMEM(flat, BF), pltpu.VMEM(flat, BF),
            pltpu.VMEM(flat, F32), pltpu.VMEM((2, 8, NX), F32), pltpu.VMEM((4, 8, NX), F32), dma((10,)), dma((10,)),
            dma((9,)),
            dma((2, 2, 3, chunks)), dma((2, 2, 3, chunks)),
            dma((2, 2, 3)), dma((2, 2, 3)), dma((2, 2, 3)), dma((2, 2, 3)),
            dma((2, 2, 3, chunks)), dma((2, 2, 3, chunks)),
        ],
        compiler_params=pltpu.CompilerParams(collective_id=1, has_side_effects=True, vmem_limit_bytes=LIMIT),
    )(forcing, weights, ytab, fwd, inv, pick, wt, cols, four, dec, turning, bias, depth)


def finish_body(final_ref, residual_ref, final_out, residual_out, sem):
    copies = [pltpu.make_async_copy(final_ref.at[pl.ds(4 * i, 4)], final_out.at[pl.ds(4 * i, 4)], sem.at[i]) for i in range(8)]
    copies.append(pltpu.make_async_copy(residual_ref, residual_out, sem.at[8]))
    for c in copies:
        c.start()
    for c in copies:
        c.wait()


def finish(final, residual):
    any_space = pl.BlockSpec(memory_space=pl.ANY)
    return pl.pallas_call(
        finish_body, name="finish", in_specs=[pl.BlockSpec(memory_space=pltpu.VMEM)] * 2, out_specs=[any_space] * 2,
        out_shape=[jax.ShapeDtypeStruct(final.shape, F32), jax.ShapeDtypeStruct(residual.shape, F32)],
        scratch_shapes=[pltpu.SemaphoreType.DMA((9,))],
        compiler_params=pltpu.CompilerParams(vmem_limit_bytes=1 << 20),
    )(final, residual)


@functools.lru_cache(None)
def kron_parts():
    order = np.arange(C).reshape(2, 8, 2).transpose(0, 2, 1).reshape(C)
    pick = np.zeros((C, C), np.float32)
    pick[np.arange(C), order] = 1.0
    spread = np.repeat(np.eye(C, dtype=np.float32), 16, 1)
    four = np.repeat(np.eye(4, dtype=np.float32), 16, 0)
    return [v.astype(BF) for v in (np.repeat(pick, 16, 0), spread, four)]


def on_device(forcing, spectral_weight, point_weight, point_bias, decoder, coriolis, layer_depth):
    source = forcing[0]
    fwd, inv = (jnp.asarray(v) for v in x_tables())
    ytab = jnp.asarray(y_tables())
    pick, cols, four = [jnp.asarray(v) for v in kron_parts()]
    final, residual = steps(source, spectral_weight, ytab, fwd, inv, pick, point_weight, cols, four, decoder,
                            coriolis[None], point_bias, layer_depth)
    final, residual = finish(final, residual)
    return final[None], residual[:, None]


def solution(mesh):
    return jax.shard_map(
        on_device,
        mesh=mesh,
        in_specs=(
            P("lev", None, "gy", None),
            P(None, "gy", None, None, None),
            P(),
            P(),
            P(),
            P("gy"),
            P(),
        ),
        out_specs=(P("lev", None, "gy", None), P(None, "lev", "gy", None)),
        check_vma=False,
    )
```

```python
import functools
import math

import jax
import jax.numpy as jnp
import numpy as np
from jax import lax
from jax.experimental import pallas as pl
from jax.experimental.pallas import tpu as pltpu
from jax.sharding import PartitionSpec as P

C = 32
NX = 1024
NY = 1536
M = 128
ROWS = 96
ITERS = 3
MESH = pl.DeviceIdType.MESH
BF = jnp.bfloat16
F32 = jnp.float32
YC = 48
LC = 48
SPLIT = 3
TILE = 256


def turns(a, b, length):
    phase = (a[:, None] * b[None, :]) % length
    return phase.astype(np.float32) * np.float32(2.0 * math.pi / length)


def lane_modes(half, order):
    p, r, s, j = np.meshgrid(np.array(order), np.arange(2), np.arange(4), np.arange(8), indexing="ij")
    k = 32 * s + 8 * p + j if half == 0 else 32 * p + 8 * s + j
    return k.reshape(-1), r.reshape(-1)


@functools.lru_cache(None)
def x_tables():
    forward, inverse = [], []
    for half in range(2):
        for order in ((0, 1, 2, 3), (1, 0, 3, 2)):
            k, r = lane_modes(half, order)
            turned = turns(np.arange(NX), k, NX)
            wave = np.where(r == 0, np.cos(turned), -np.sin(turned)).astype(np.float32)
            factor = np.where(k == 0, 1.0, 2.0).astype(np.float32) / np.float32(NX * NY)
            forward.append(wave)
            inverse.append((wave * factor[None, :]).T)
    return np.stack(forward).astype(BF), np.stack(inverse).astype(BF)


@functools.lru_cache(None)
def y_tables():
    m = np.arange(M)
    signed = np.where(m < M // 2, m, m + NY - M)
    rows = np.arange(NY)
    turned = turns(rows, signed, NY)
    both = np.concatenate([np.cos(turned), np.sin(turned)], 1).astype(np.float32).astype(BF)
    blocks = both.reshape(4, 4, ROWS, 2 * M)
    first = blocks.reshape(4, 4 * ROWS, 2 * M)
    second = blocks.transpose(1, 0, 2, 3).reshape(4, 4 * ROWS, 2 * M)
    return np.stack([first, second])


def gelu(v):
    inner = v * (math.sqrt(2.0 / math.pi) + (math.sqrt(2.0 / math.pi) * 0.044715) * (v * v))
    return (0.5 * v) * (1.0 + jnp.tanh(inner))


def lane_mask(rows):
    return lax.broadcasted_iota(jnp.int32, (rows, 128), 1) < 64


SMEM = pl.BlockSpec(memory_space=pltpu.SMEM)
LIMIT = 42 << 20


def shifted(field, step, axis):
    return pltpu.roll(field, step % field.shape[axis], axis)


def diff_x(field):
    return (shifted(field, -1, 1) - shifted(field, 1, 1)) * 0.5


def diff_y(field, before, after):
    at = lax.broadcasted_iota(jnp.int32, field.shape, 0)
    upper = jnp.where(at == field.shape[0] - 1, after, shifted(field, -1, 0))
    lower = jnp.where(at == 0, before, shifted(field, 1, 0))
    return (upper - lower) * 0.5


def tail_peers():
    lev = lax.axis_index("lev")
    g = lax.axis_index("gy")
    x, c = lev // 2, lev % 2
    beside = {"lev": (lev + 1 + 6 * (1 - c)) % 8}
    near_by = [{"lev": 2 * x + 1 - c}, beside, {"gy": (g + 1) % 16}, {"gy": (g + 15) % 16}]
    return near_by + [{"lev": (lev + 2 * d) % 8} for d in range(1, 4)]


def tail_body(fields_ref, turning_ref, depth_ref, out_ref, own, other, chip, lower, total, share, up_out, up_in,
              geo, edge_out, edge_in, ss, rs):
    lev = lax.axis_index("lev")
    g = lax.axis_index("gy")
    x, c = lev // 2, lev % 2
    partner = {"lev": 2 * x + 1 - c}
    next_row, last_row = {"gy": (g + 1) % 16}, {"gy": (g + 15) % 16}

    def copy(src, dst, at, peer):
        return pltpu.make_async_remote_copy(src_ref=src, dst_ref=dst, send_sem=ss.at[at], recv_sem=rs.at[at],
                                            device_id=peer, device_id_type=MESH)

    spot = lax.broadcasted_iota(jnp.int32, (ROWS, ROWS), 0) == lax.broadcasted_iota(jnp.int32, (ROWS, ROWS), 1)
    turning = jnp.sum(jnp.where(spot, jnp.broadcast_to(turning_ref[...], (ROWS, ROWS)), 0.0), 1, keepdims=True)
    half = pl.ds(pl.multiple_of(48 * c, 48), 48)
    rest = pl.ds(pl.multiple_of(48 * (1 - c), 48), 48)
    weighted = fields_ref[3] * depth_ref[lev]
    own[...] = weighted.astype(BF)
    up_out[...] = fields_ref[2].astype(BF)
    edge_out[0] = fields_ref[1, 88:96]
    edge_out[1] = fields_ref[1, 0:8]
    all_rows = copy(own, other, 0, partner)
    some_rows = copy(own.at[0:48], other.at[0:48], 0, partner)

    @pl.when(c == 0)
    def _():
        all_rows.start()

    @pl.when(c == 1)
    def _():
        some_rows.start()

    winds = [copy(edge_out.at[0], edge_in.at[0], 1, next_row), copy(edge_out.at[1], edge_in.at[1], 2, last_row)]
    for w in winds:
        w.start()

    @pl.when(c == 0)
    def _():
        all_rows.wait_send()
        some_rows.wait_recv()

    @pl.when(c == 1)
    def _():
        some_rows.wait_send()
        all_rows.wait_recv()

    chip[...] = (own[half, :].astype(F32) + other[half, :].astype(F32)).astype(BF)
    sums = [copy(chip, lower.at[d - 1], 2 + d, {"lev": (lev + 2 * d) % 8}) for d in range(1, 4)]
    for d in range(1, 4):
        @pl.when(x + d <= 3)
        def _():
            sums[d - 1].start()

    rising = copy(up_out, up_in, 6, {"lev": (lev + 1) % 8})

    @pl.when(lev < 7)
    def _():
        rising.start()

    for w in winds:
        w.wait()
    east, north = fields_ref[0], fields_ref[1]
    out_ref[0] = diff_x(east) + diff_y(north, edge_in[0, 7:8], edge_in[1, 0:1]) + fields_ref[2]
    total[half, :] = jnp.zeros((48, NX), F32)
    for d in range(1, 4):
        @pl.when(x >= d)
        def _():
            sums[d - 1].wait_recv()
            total[half, :] += lower[d - 1].astype(F32)

    share[...] = total[half, :]
    shared = copy(share, total.at[half], 7, partner)
    shared.start()

    @pl.when(lev >= 1)
    def _():
        rising.wait_recv()
        out_ref[0] -= up_in[...].astype(F32)

    shared.wait()
    geo[...] = total[...] + fields_ref[3] * depth_ref[lev]

    @pl.when(c == 1)
    def _():
        geo[...] += other[...].astype(F32)

    edges = [copy(geo.at[88:96], edge_in.at[2], 8, next_row), copy(geo.at[0:8], edge_in.at[3], 9, last_row)]
    for e in edges:
        e.start()
    out_ref[1] = turning * north - diff_x(geo[...])
    for e in edges:
        e.wait()
    out_ref[2] = turning * east + diff_y(geo[...], edge_in[2, 7:8], edge_in[3, 0:1])
    for d in range(1, 4):
        @pl.when(x + d <= 3)
        def _():
            sums[d - 1].wait_send()

    @pl.when(lev < 7)
    def _():
        rising.wait_send()


def dot_last(left, right):
    return lax.dot_general(left, right, (((1,), (1,)), ((), ())), preferred_element_type=F32)


def kron_values(left, cols):
    left = left.astype(BF)
    full = jnp.dot(left, cols, preferred_element_type=F32)
    i = lax.broadcasted_iota(jnp.int32, full.shape, 0) % 16
    j = lax.broadcasted_iota(jnp.int32, full.shape, 1) % 16
    return jnp.where(i == j, full, 0.0).astype(BF)


def steps_body(forcing_ref, weight_ref, ytab_ref, fwd_hbm, inv_hbm, pick_ref, wt_ref, cols_ref, four_ref, dec_ref,
               turning_ref, bias_ref, depth_ref, final, out_ref,
               source, state, fwd, inv, kron, wbuf, tabs, near, r1, part, s2, r2, sp, mx, r3, m2, s4, back,
               dmat, fields, own_heat, other_heat, chip, lower, total, share, up_out, up_in, geo,
               edge_out, edge_in, ts, tr, lsem, s1s, s1r, s2s, s2r, s3s, s3r, s4s, s4r):
    g = lax.axis_index("gy")
    z, y = g // 4, g % 4
    own = ((y, z), (z, y))

    def first_peer(h, a):
        return {"gy": z * 4 + a} if h == 0 else {"gy": a * 4 + y}

    def second_peer(h, b):
        return {"gy": b * 4 + y} if h == 0 else {"gy": z * 4 + b}

    barrier = pltpu.get_barrier_semaphore()
    for h in range(2):
        for d in range(1, 4):
            pl.semaphore_signal(barrier, 1, device_id=first_peer(h, (own[h][0] + d) % 4), device_id_type=MESH)

    for peer in tail_peers():
        pl.semaphore_signal(barrier, 1, device_id=peer, device_id_type=MESH)

    def rows_of(k):
        return pl.ds(pl.multiple_of(k * YC, YC), YC)

    def few_of(k):
        return pl.ds(pl.multiple_of(k * LC, LC), LC)

    chunks = ROWS // YC
    pieces = ROWS // LC

    def local(src, dst, at):
        return pltpu.make_async_copy(src, dst, lsem.at[at])

    load_fwd = local(fwd_hbm, fwd, 0)
    load_source = [local(forcing_ref.at[:, rows_of(k)], source.at[:, rows_of(k)], 1 + k) for k in range(chunks)]
    load_tabs = [local(ytab_ref.at[h, own[h][1]], tabs.at[h], 4 + h) for h in range(2)]
    load_weights = local(weight_ref, wbuf, 6)
    load_inv = local(inv_hbm, inv, 7)
    load_state = local(forcing_ref, state, 8)
    for c in [load_fwd, *load_source, *load_tabs, load_weights, load_inv, load_state]:
        c.start()

    def remote(src, dst, send, recv, peer):
        return pltpu.make_async_remote_copy(src_ref=src, dst_ref=dst, send_sem=send, recv_sem=recv, device_id=peer,
                                            device_id_type=MESH)

    def lanes_of(e):
        return slice(512 * e, 512 * e + 512)

    def one(h, d, k, e):
        a = own[h][0]
        return remote(near.at[h, (a + d) % 4, few_of(k), lanes_of(e)], r1.at[h, a, few_of(k), lanes_of(e)],
                      s1s.at[e, h, d - 1, k], s1r.at[e, h, d - 1, k], first_peer(h, (a + d) % 4))

    def two(h, d, e):
        b = own[h][1]
        at = pl.ds(8 * e, 8)
        return remote(s2.at[h, (b + d) % 4, at], r2.at[h, d - 1, at], s2s.at[e, h, d - 1], s2r.at[e, h, d - 1],
                      second_peer(h, (b + d) % 4))

    def three(h, d, e):
        b = own[h][1]
        at = pl.ds(8 * e, 8)
        return remote(r3.at[h, b, at], r3.at[h, b, at], s3s.at[e, h, d - 1], s3r.at[e, h, d - 1],
                      second_peer(h, (b + d) % 4))

    def four(h, d, k, e):
        a = own[h][0]
        return remote(s4.at[h, (a + d) % 4, rows_of(k), lanes_of(e)], back.at[h, a, rows_of(k), lanes_of(e)],
                      s4s.at[e, h, d - 1, k], s4r.at[e, h, d - 1, k], first_peer(h, (a + d) % 4))

    def forward(k, load, e):
        rows = few_of(k)
        mask = lane_mask(LC)
        for h in range(2):
            outs = []
            for par in range(2):
                lhs = jnp.concatenate([load(16 * h + 2 * pair + par, rows) for pair in range(4 * e, 4 * e + 4)], 0)
                outs.append(jnp.dot(lhs, fwd[2 * h + par], preferred_element_type=F32))
            even, odd = outs
            for pair in range(4 * e, 4 * e + 4):
                at = slice((pair - 4 * e) * LC, (pair - 4 * e + 1) * LC)
                for v in range(2):
                    lo = even[at, 128 * v:128 * v + 128]
                    hi = odd[at, 128 * v:128 * v + 128]
                    lanes = slice(128 * pair, 128 * pair + 128)
                    near[h, 2 * v, rows, lanes] = jnp.where(mask, lo, hi).astype(BF)
                    near[h, 2 * v + 1, rows, lanes] = jnp.where(mask, hi, lo).astype(BF)
            for d in range(1, 4):
                one(h, d, k, e).start()
            a = own[h][0]
            r1[h, a, rows, lanes_of(e)] = near[h, a, rows, lanes_of(e)]

    def update(k, sink, e):
        rows = few_of(k)
        mask = lane_mask(LC)
        groups = []
        for h in range(2):
            even, odd = [], []
            for pair in range(4 * e, 4 * e + 4):
                b = [back[h, p, rows, 128 * pair:128 * pair + 128] for p in range(4)]
                even.append(jnp.concatenate([jnp.where(mask, b[0], b[1]), jnp.where(mask, b[2], b[3])], 1))
                odd.append(jnp.concatenate([jnp.where(mask, b[1], b[0]), jnp.where(mask, b[3], b[2])], 1))
            groups.append(jnp.concatenate(even, 0))
            groups.append(jnp.concatenate(odd, 0))
        for t in range(NX // TILE):
            cols = slice(t * TILE, (t + 1) * TILE)
            for q in range(4):
                h, par = q // 2, q % 2
                spread = jnp.dot(groups[q], inv[q, :, cols], preferred_element_type=F32)
                spread = spread.reshape(4, LC, TILE)
                for pair in range(4 * e, 4 * e + 4):
                    c = 16 * h + 2 * pair + par
                    sink(q, pair, c, rows, cols, gelu(final[c, rows, cols] + spread[pair - 4 * e]))

    def prepare(first, last):
        @pl.loop(first, last)
        def _(k):
            rows = pl.ds(pl.multiple_of(16 * k, 16), 16)
            for t in range(NX // TILE):
                cols = slice(t * TILE, (t + 1) * TILE)
                st = state[:, rows, cols].reshape(C * 16, TILE)
                mixed = jnp.dot(kron[...], st, preferred_element_type=F32).reshape(4, 8, 16, TILE)
                for q in range(4):
                    for pair in range(8):
                        c = 16 * (q // 2) + 2 * pair + q % 2
                        final[c, rows, cols] = mixed[q, pair] + (source[c, rows, cols].astype(F32) + bias_ref[c])

    def keep_state(q, pair, c, rows, cols, value):
        state[c, rows, cols] = value.astype(BF)

    def keep_final(q, pair, c, rows, cols, value):
        final[c, rows, cols] = value
        state[c, rows, cols] = value.astype(BF)

    pl.semaphore_wait(barrier, 13)
    load_fwd.wait()

    @pl.loop(0, chunks)
    def _(k):
        pltpu.make_async_copy(forcing_ref.at[:, rows_of(k)], source.at[:, rows_of(k)], lsem.at[1 + k]).wait()
        pl.loop(0, YC // LC)(lambda t: [forward(k * (YC // LC) + t, lambda c, rows: source[c, rows], e) for e in range(2)] and None)

    kron[...] = kron_values(dot_last(pick_ref[...], wt_ref[...]), cols_ref[...])
    dmat[...] = kron_values(jnp.dot(four_ref[...], dec_ref[...], preferred_element_type=F32), cols_ref[...])
    for c in [*load_tabs, load_weights, load_inv, load_state]:
        c.wait()

    @pl.loop(0, ITERS)
    def _(it):
        for e in range(2):
            for h in range(2):
                a = own[h][0]
                for k in range(pieces):
                    for d in range(1, 4):
                        one(h, d, k, e).wait()

                @pl.loop(2 * e, 2 * e + 2)
                def _(n):
                    cols = pl.ds(pl.multiple_of(n * 256, 256), 256)
                    x = r1[h, :, :, cols].reshape(4 * ROWS, 256)
                    pt = lax.dot_general(x, tabs[h], (((0,), (0,)), ((), ())), preferred_element_type=F32)
                    pt = pt.reshape(2, 2, 2, 4, 8, 256)
                    for pair in range(2):
                        for h2 in range(2):
                            q0, q1 = pt[pair, h2, 0], pt[pair, h2, 1]
                            re = q0[..., :M] + q1[..., M:]
                            im = q1[..., :M] - q0[..., M:]
                            both = jnp.concatenate([re, im], 1)
                            c = 2 * (2 * n + pair) + lax.rem(h2 + a, 2)
                            part[h, :, c] = both
                            s2[h, :, c] = both.astype(BF)

                for d in range(1, 4):
                    two(h, d, e).start()

        prepare(0, SPLIT)
        for e, h in ((0, 0), (0, 1), (1, 0), (1, 1)):
            b = own[h][1]
            for d in range(1, 4):
                two(h, d, e).wait()

            @pl.loop(8 * e, 8 * e + 8)
            def _(c):
                total = part[h, b, c]
                for d in range(3):
                    total = total + r2[h, d, c].astype(F32)
                sp[16 * h + c] = total

            for oh in range(2):
                outs = pl.ds(16 * oh, 16)
                for j in range(8):
                    def add(i, acc):
                        ar, ai = acc
                        wr = wbuf[0, j, i, outs].astype(F32)
                        wi = wbuf[1, j, i, outs].astype(F32)
                        sr = jnp.broadcast_to(sp[i, pl.ds(j, 1), :], (16, M))
                        si = jnp.broadcast_to(sp[i, pl.ds(8 + j, 1), :], (16, M))
                        return ar + (sr * wr - si * wi), ai + (sr * wi + si * wr)

                    re_at, im_at = pl.ds(j, 16, stride=16), pl.ds(8 + j, 16, stride=16)
                    if e == 0 and h == 0:
                        begin = (jnp.zeros((16, M), F32), jnp.zeros((16, M), F32))
                    else:
                        begin = (mx[oh, re_at, :], mx[oh, im_at, :])
                    ar, ai = lax.fori_loop(16 * h + 8 * e, 16 * h + 8 * e + 8, add, begin, unroll=8)
                    mx[oh, re_at, :] = ar
                    mx[oh, im_at, :] = ai
                if e == 1 and h == 1:
                    r3[oh, own[oh][1]] = mx[oh].reshape(16, 16, M).astype(BF)
                    for late in range(2):
                        for d in range(1, 4):
                            three(oh, d, late).start()

        prepare(SPLIT, 6)

        def back_chunk(h, k, e):
            rows = rows_of(k)
            a = own[h][0]
            left = jnp.concatenate([tabs[h, pl.ds(pl.multiple_of(ROWS * p + k * YC, YC), YC)] for p in range(4)], 0)
            for n in range(2 * e, 2 * e + 2):
                lanes = slice(256 * n, 256 * n + 256)
                out = lax.dot_general(left, m2[h, lanes], (((1,), (1,)), ((), ())), preferred_element_type=F32)
                s4[h, :, rows, lanes] = out.reshape(4, YC, 256).astype(BF)
            for d in range(1, 4):
                four(h, d, k, e).start()
            back[h, a, rows, lanes_of(e)] = s4[h, a, rows, lanes_of(e)]

        for e in range(2):
            for h in range(2):
                a = own[h][0]
                for d in range(1, 4):
                    three(h, d, e).wait()

                @pl.loop(4 * e, 4 * e + 4)
                def _(n):
                    rows = []
                    for h2 in range(2):
                        c = 2 * n + lax.rem(h2 + a, 2)
                        block = r3[h, :, c].astype(F32).reshape(4, 2, 8, M)
                        re = block[:, 0].reshape(32, M)
                        im = block[:, 1].reshape(32, M)
                        rows.append(jnp.concatenate([re, -im], 1))
                        rows.append(jnp.concatenate([im, re], 1))
                    m2[h, pl.ds(pl.multiple_of(n * 128, 128), 128)] = jnp.concatenate(rows, 0).astype(BF)

                back_chunk(h, 0, e)

            @pl.loop(1, chunks)
            def _(k):
                for h in range(2):
                    back_chunk(h, k, e)

        @pl.when(it < ITERS - 1)
        def _():
            for e in range(2):
                @pl.loop(0, chunks)
                def _(k):
                    for h in range(2):
                        for d in range(1, 4):
                            four(h, d, k, e).wait()
                    update(k, keep_state, e)
                    forward(k, lambda c, rows: state[c, rows], e)

    for e in range(2):
        @pl.loop(0, chunks)
        def _(k):
            for h in range(2):
                for d in range(1, 4):
                    four(h, d, k, e).wait()
            update(k, keep_final, e)
            if e == 1:
                for s in range(YC // 16):
                    rows = pl.ds(pl.multiple_of(k * YC + 16 * s, 16), 16)
                    f = jnp.dot(dmat[...], state[:, rows, :].reshape(C * 16, NX), preferred_element_type=F32)
                    fields[:, rows, :] = f.reshape(4, 16, NX)

    tail_body(fields, turning_ref, depth_ref, out_ref, own_heat, other_heat, chip, lower, total, share, up_out, up_in,
              geo, edge_out, edge_in, ts, tr)


def steps(forcing, weights, ytab, fwd, inv, pick, wt, cols, four, dec, turning, bias, depth):
    near_shape = (2, 4, ROWS, NX)
    chunks = ROWS // YC
    flat = (ROWS, NX)
    any_space = pl.BlockSpec(memory_space=pl.ANY)
    vmem = pl.BlockSpec(memory_space=pltpu.VMEM)
    dma = pltpu.SemaphoreType.DMA
    return pl.pallas_call(
        steps_body, name="steps",
        in_specs=[any_space] * 5 + [vmem] * 6 + [SMEM] * 2,
        out_specs=[vmem, vmem],
        out_shape=[pltpu.VMEM((C, ROWS, NX), F32), pltpu.VMEM((3, ROWS, NX), F32)],
        scratch_shapes=[
            pltpu.VMEM((C, ROWS, NX), BF),
            pltpu.VMEM((C, ROWS, NX), BF),
            pltpu.VMEM(fwd.shape, BF),
            pltpu.VMEM(inv.shape, BF),
            pltpu.VMEM((C * 16, C * 16), BF),
            pltpu.VMEM((2, 8, C, C, M), BF),
            pltpu.VMEM((2, 4 * ROWS, 2 * M), BF),
            pltpu.VMEM(near_shape, BF),
            pltpu.VMEM(near_shape, BF),
            pltpu.VMEM((2, 4, 16, 16, M), F32),
            pltpu.VMEM((2, 4, 16, 16, M), BF),
            pltpu.VMEM((2, 3, 16, 16, M), BF),
            pltpu.VMEM((C, 16, M), F32),
            pltpu.VMEM((2, 16 * 16, M), F32),
            pltpu.VMEM((2, 4, 16, 16, M), BF),
            pltpu.VMEM((2, NX, 2 * M), BF),
            pltpu.VMEM(near_shape, BF),
            pltpu.VMEM(near_shape, BF),
            pltpu.VMEM((64, C * 16), BF),
            pltpu.VMEM((4, ROWS, NX), F32),
            pltpu.VMEM(flat, BF), pltpu.VMEM(flat, BF), pltpu.VMEM((48, NX), BF), pltpu.VMEM((3, 48, NX), BF),
            pltpu.VMEM(flat, F32), pltpu.VMEM((48, NX), F32), pltpu.VMEM(flat, BF), pltpu.VMEM(flat, BF),
            pltpu.VMEM(flat, F32), pltpu.VMEM((2, 8, NX), F32), pltpu.VMEM((4, 8, NX), F32), dma((10,)), dma((10,)),
            dma((9,)),
            dma((2, 2, 3, chunks)), dma((2, 2, 3, chunks)),
            dma((2, 2, 3)), dma((2, 2, 3)), dma((2, 2, 3)), dma((2, 2, 3)),
            dma((2, 2, 3, chunks)), dma((2, 2, 3, chunks)),
        ],
        compiler_params=pltpu.CompilerParams(collective_id=1, has_side_effects=True, vmem_limit_bytes=LIMIT),
    )(forcing, weights, ytab, fwd, inv, pick, wt, cols, four, dec, turning, bias, depth)


def finish_body(final_ref, residual_ref, final_out, residual_out, sem):
    copies = [pltpu.make_async_copy(final_ref.at[pl.ds(4 * i, 4)], final_out.at[pl.ds(4 * i, 4)], sem.at[i]) for i in range(8)]
    copies.append(pltpu.make_async_copy(residual_ref, residual_out, sem.at[8]))
    for c in copies:
        c.start()
    for c in copies:
        c.wait()


def finish(final, residual):
    any_space = pl.BlockSpec(memory_space=pl.ANY)
    return pl.pallas_call(
        finish_body, name="finish", in_specs=[pl.BlockSpec(memory_space=pltpu.VMEM)] * 2, out_specs=[any_space] * 2,
        out_shape=[jax.ShapeDtypeStruct(final.shape, F32), jax.ShapeDtypeStruct(residual.shape, F32)],
        scratch_shapes=[pltpu.SemaphoreType.DMA((9,))],
        compiler_params=pltpu.CompilerParams(vmem_limit_bytes=1 << 20),
    )(final, residual)


@functools.lru_cache(None)
def kron_parts():
    order = np.arange(C).reshape(2, 8, 2).transpose(0, 2, 1).reshape(C)
    pick = np.zeros((C, C), np.float32)
    pick[np.arange(C), order] = 1.0
    spread = np.repeat(np.eye(C, dtype=np.float32), 16, 1)
    four = np.repeat(np.eye(4, dtype=np.float32), 16, 0)
    return [v.astype(BF) for v in (np.repeat(pick, 16, 0), spread, four)]


def on_device(forcing, spectral_weight, point_weight, point_bias, decoder, coriolis, layer_depth):
    source = forcing[0]
    fwd, inv = (jnp.asarray(v) for v in x_tables())
    ytab = jnp.asarray(y_tables())
    pick, cols, four = [jnp.asarray(v) for v in kron_parts()]
    final, residual = steps(source, spectral_weight, ytab, fwd, inv, pick, point_weight, cols, four, decoder,
                            coriolis[None], point_bias, layer_depth)
    final, residual = finish(final, residual)
    return final[None], residual[:, None]


def solution(mesh):
    return jax.shard_map(
        on_device,
        mesh=mesh,
        in_specs=(
            P("lev", None, "gy", None),
            P(None, "gy", None, None, None),
            P(),
            P(),
            P(),
            P("gy"),
            P(),
        ),
        out_specs=(P("lev", None, "gy", None), P(None, "lev", "gy", None)),
        check_vma=False,
    )
```
